128 devices in a mesh: row: 16 (over y_lo, z, core), col: 8 (over x, y_hi).
Axes of the slice: x: 4, y: 4 (y_hi: 2, y_lo: 2; y = y_hi * 2 + y_lo), z: 4, core: 2. Of those that a mesh axis runs over, the one named last changes fastest.
Arguments:
- density: bfloat16 [2, 8192, 8192], P(None, 'row', 'col'), may hold values from -6 to 6
- kraus: bfloat16 [3, 2, 2, 512, 512], replicated, may hold values from -0.1875 to 0.1875
- targets: int32 [3, 9], replicated, may hold values from 0 to 8, each once within a row
Outputs:
- evolved: bfloat16 [2, 8192, 8192], P(None, 'row', 'col')
The draws below stay inside these ranges and needn't reach their ends.
Inputs may be any that keep to these rules, and one draw needn't show every extreme that they name: Each row of targets names each of the 9 qubits once.
All inputs are finite; a program needn't handle non-finite values.
Results may differ from the reference program's by a relative error of at most 0.012.
Values may be sent and summed in bfloat16 or wider, within the bound.
No kernel may reach another device: no remote copies, remote signals or barrier semaphores. Data moves between devices by JAX's collectives and lax.ppermute only.
A program may use at most 64 MiB of HBM per device.

```python
import jax
import jax.numpy as jnp

DIM = 8192
STATES = 512
QUBITS = 9
SECTIONS = 3
KRAUS = 2
ROW_DEV = 512
N_ROW = 16


def level_of(stream_key, extent, shards, low, largest):
    gain, own = 1.0, jax.random.fold_in(stream_key, 6)
    for dim, blocks in shards:
        steps = jnp.exp(jax.random.uniform(jax.random.fold_in(own, dim), (blocks,), jnp.float32, low / len(shards), largest / len(shards)))
        gain = gain * jnp.repeat(steps, extent[dim] // blocks).reshape([-1 if axis == dim else 1 for axis in range(len(extent))])
    return gain


def noise(key, shape, width, bound, shards=(), held_as=jnp.bfloat16):
    factor_of = level_of(key, shape, shards, -0.22, 0.18) if shards else 1.0
    drawn = jax.random.normal(key, shape, jnp.float32) * width * factor_of
    return jnp.minimum(jnp.maximum(drawn, -bound), bound).astype(held_as)


def setup_inputs(seed: int = 0) -> dict:
    arg_keys = jax.random.split(jax.random.key(seed), 4)
    density = noise(arg_keys[0], (2, DIM, DIM), 1.0, 6.0, ((1, 16), (2, 8)))
    kraus = noise(arg_keys[1], (SECTIONS, KRAUS, 2, STATES, STATES), (2 * STATES) ** -0.5, 0.1875)
    targets = jax.vmap(lambda own: jax.random.permutation(own, QUBITS))(jax.random.split(arg_keys[2], SECTIONS)).reshape((SECTIONS, QUBITS)).astype(jnp.int32)
    return {"density": density, "kraus": kraus, "targets": targets}


def regroup(state, axis_dim):
    length = state.shape[axis_dim]
    inner = (N_ROW, N_ROW, length // (N_ROW * N_ROW))
    blocks = state.reshape(state.shape[:axis_dim] + inner + state.shape[axis_dim + 1:])
    return jnp.swapaxes(blocks, axis_dim, axis_dim + 1).reshape(state.shape)


def swap_bits(state, axis_dim, high, low):
    length = state.shape[axis_dim]
    inner = (length // (2 * high), 2, high // (2 * low), 2, low)
    halves = state.reshape(state.shape[:axis_dim] + inner + state.shape[axis_dim + 1:])
    return jnp.swapaxes(halves, axis_dim + 1, axis_dim + 3).reshape(state.shape)


def qubit_order(target_row):
    states = jnp.arange(STATES, dtype=jnp.int32)
    bits = (states[:, None] >> target_row[None, :].astype(jnp.int32)) & 1
    powers = (2 ** jnp.arange(QUBITS, dtype=jnp.int32)).astype(jnp.int32)
    return jnp.sum(bits * powers[None, :], axis=1).astype(jnp.int32)


def row_apply(operator, state):
    real_part, imag_part = operator[0], operator[1]
    stacked = jnp.stack([jnp.stack([real_part, -imag_part]), jnp.stack([imag_part, real_part])])
    parts, rows, cols = state.shape
    blocks = state.reshape(parts, rows // STATES, STATES, cols)
    result = jnp.einsum("pqmn,qbnc->pbmc", stacked.astype(jnp.float32), blocks.astype(jnp.float32))
    return result.reshape(state.shape).astype(jnp.bfloat16)


def col_apply(operator, state):
    real_t, imag_t = operator[0].T, operator[1].T
    stacked = jnp.stack([jnp.stack([real_t, -imag_t]), jnp.stack([imag_t, real_t])])
    parts, rows, cols = state.shape
    blocks = state.reshape(parts, rows, cols // STATES, STATES)
    result = jnp.einsum("qibn,qpnm->pibm", blocks.astype(jnp.float32), stacked.astype(jnp.float32))
    return result.reshape(state.shape)


def reference(density, kraus, targets):
    state = regroup(regroup(density, 1), 2)
    for section in range(SECTIONS):
        order_map = qubit_order(targets[section])
        acting = jnp.take(jnp.take(kraus[section], order_map, axis=2), order_map, axis=3)
        state = swap_bits(state, 1, ROW_DEV * 2 ** section, STATES // 2)
        state = swap_bits(state, 2, ROW_DEV * 2 ** section, STATES // 2)
        total = jnp.zeros(state.shape, jnp.float32)
        for term in range(KRAUS):
            left = row_apply(acting[term], state)
            total = total + col_apply(acting[term], left)
        state = total.astype(jnp.bfloat16)
    return state
```

```python
import jax
import jax.numpy as jnp
from jax import lax
from jax.experimental import pallas as pl
from jax.experimental.pallas import tpu as pltpu
from jax.sharding import Mesh
from jax.sharding import PartitionSpec as P

STATES = 512
QUBITS = 9
SECTIONS = 3
HALF = 256
BF16 = jnp.bfloat16
F32 = jnp.float32
AXES = ("ylo", "z1", "z0", "core", "x1", "x0", "yhi")
GATHERED = ("z1", "z0", "core", "x0", "yhi")
CORE, X1, Z1, X0, YHI = range(5)
VMEM = 48 * 2**20


def cost(flops, data):
    return pl.CostEstimate(flops=flops, bytes_accessed=data, transcendentals=0)


def pack(density):
    def kernel(x_ref, o_ref):
        for col in range(4):
            low, high = col >> 1, col & 1
            for top in range(2):
                tile = top * 4 + high * 2 + low
                o_ref[0, col, :, :, top * 128 : top * 128 + 128] = x_ref[:, :, tile * 128 : tile * 128 + 128]

    return pl.pallas_call(
        kernel,
        grid=(2, 2, 2),
        in_specs=[pl.BlockSpec((2, 64, 1024), lambda b7, b8, b6: (0, b8 * 4 + b7 * 2 + b6, 0))],
        out_specs=pl.BlockSpec((1, 4, 2, 64, 256), lambda b7, b8, b6: (b7 * 4 + b8 * 2 + b6, 0, 0, 0, 0)),
        out_shape=jax.ShapeDtypeStruct((8, 4, 2, 64, 256), BF16),
        cost_estimate=cost(0, 2**22),
        name="pack",
    )(density)


def operators(kraus, targets):
    def kernel(t_ref, k_ref, o_ref):
        section = pl.program_id(0)

        def order(state):
            total = jnp.zeros_like(state)
            for bit in range(QUBITS):
                total += ((state >> t_ref[section, bit]) & 1) << bit
            return total

        out_state = lax.broadcasted_iota(jnp.int32, (STATES, 1), 0)
        place = lax.broadcasted_iota(jnp.int32, (1, STATES), 1)
        mixed = ((place >> 5 & 1) << 8) | ((place >> 6 & 7) << 5) | (place & 31)
        in_state = jnp.where(section == 0, mixed, place)
        lanes = lax.broadcasted_iota(jnp.int32, (STATES, STATES), 1)
        rows = lax.broadcasted_iota(jnp.int32, (STATES, STATES), 0)
        left = (order(out_state) == lanes).astype(F32).astype(BF16)
        right = (order(in_state) == rows).astype(F32).astype(BF16)
        for term in range(2):
            for part in range(2):
                picked = jnp.dot(left, k_ref[0, term, part], preferred_element_type=F32).astype(BF16)
                at = (term * 2 + part) * STATES
                o_ref[0, :, at : at + STATES] = jnp.dot(picked, right, preferred_element_type=F32).astype(BF16)

    return pl.pallas_call(
        kernel,
        grid=(SECTIONS,),
        in_specs=[
            pl.BlockSpec(memory_space=pltpu.SMEM),
            pl.BlockSpec((1, 2, 2, STATES, STATES), lambda s: (s, 0, 0, 0, 0)),
        ],
        out_specs=pl.BlockSpec((1, STATES, 4 * STATES), lambda s: (s, 0, 0)),
        out_shape=jax.ShapeDtypeStruct((SECTIONS, STATES, 4 * STATES), BF16),
        compiler_params=pltpu.CompilerParams(vmem_limit_bytes=VMEM),
        cost_estimate=cost(24 * 2 * 512**3, 12 * 2**20),
        name="operators",
    )(targets, kraus)


def channel(x, w_ref, lhs_ref, emit):
    for tile in range(2):
        for part in range(2):
            if part == 0:
                columns = jnp.concatenate([x(tile, 0), -x(tile, 1)], axis=0)
            else:
                columns = jnp.concatenate([x(tile, 1), x(tile, 0)], axis=0)
            for term in range(2):
                product = jnp.dot(
                    w_ref[0, :, term * 1024 : term * 1024 + 1024], columns, preferred_element_type=F32
                ).astype(BF16)
                at = term * 1024 + part * STATES + tile * HALF
                lhs_ref[0:STATES, at : at + HALF] = product
                other = term * 1024 + (1 - part) * STATES + tile * HALF
                lhs_ref[STATES:, other : other + HALF] = product if part else -product
    for tile in range(2):
        total = lax.dot_general(
            lhs_ref[...],
            w_ref[0, tile * HALF : tile * HALF + HALF, :],
            (((1,), (1,)), ((), ())),
            preferred_element_type=F32,
        )
        emit(tile, total.astype(BF16))


def first_section(pos, arrived, weights):
    def kernel(pos_ref, a_ref, w_ref, keep_ref, send_ref, x_ref, lhs_ref, out_ref):
        step = pl.program_id(0)

        @pl.when(step == 0)
        def _():
            for source in range(8):
                for col in range(4):
                    for part in range(2):
                        low = a_ref[source, col, part, :, 0:128]
                        high = a_ref[source, col, part, :, 128:256]
                        rows = slice(source * 64, source * 64 + 64)
                        lanes = slice((col & 1) * 128, (col & 1) * 128 + 128)
                        x_ref[0, col >> 1, part, rows, lanes] = jnp.concatenate([low[:, :64], high[:, :64]], axis=1)
                        x_ref[1, col >> 1, part, rows, lanes] = jnp.concatenate([low[:, 64:], high[:, 64:]], axis=1)

        core = pos_ref[CORE]

        def emit(tile, value):
            out_ref[...] = value.reshape(2, 2, HALF, HALF)
            keep_ref[tile] = out_ref[:, core]
            send_ref[tile] = out_ref[:, 1 - core]

        channel(lambda tile, part: x_ref[step, tile, part], w_ref, lhs_ref, emit)

    half = jax.ShapeDtypeStruct((2, 2, HALF, STATES), BF16)
    return pl.pallas_call(
        kernel,
        grid_spec=pltpu.PrefetchScalarGridSpec(
            num_scalar_prefetch=1,
            grid=(2,),
            in_specs=[
                pl.BlockSpec((8, 4, 2, 64, 256), lambda h, pos: (0, 0, 0, 0, 0)),
                pl.BlockSpec((1, STATES, 4 * STATES), lambda h, pos: (0, 0, 0)),
            ],
            out_specs=[pl.BlockSpec((2, 2, HALF, HALF), lambda h, pos: (0, 0, 0, h))] * 2,
            scratch_shapes=[
                pltpu.VMEM((2, 2, 2, STATES, HALF), BF16),
                pltpu.VMEM((2 * STATES, 4 * STATES), BF16),
                pltpu.VMEM((2, 2, HALF, HALF), BF16),
            ],
        ),
        out_shape=[half, half],
        compiler_params=pltpu.CompilerParams(vmem_limit_bytes=VMEM),
        cost_estimate=cost(8 * 2**30, 6 * 2**20),
        name="section_0",
    )(pos, arrived, weights)


def second_section(pos, kept, arrived, weights, turn):
    def kernel(pos_ref, k_ref, a_ref, w_ref, o00, o01, o10, o11, x_ref, lhs_ref, out_ref):
        core, z1, x0 = pos_ref[CORE], pos_ref[Z1], pos_ref[X0]
        for tile in range(2):
            for part in range(2):
                lanes = slice(tile * HALF, tile * HALF + HALF)
                x_ref[tile, part, core] = k_ref[0, part, :, lanes]
                x_ref[tile, part, 1 - core] = a_ref[0, part, :, lanes]

        def emit(tile, value):
            out_ref[tile] = value.reshape(2, 2, HALF, HALF)

        channel(lambda tile, part: x_ref[tile, part].reshape(STATES, HALF), w_ref, lhs_ref, emit)
        for d, o_ref in enumerate((o00, o01, o10, o11)):
            o_ref[...] = out_ref[x0 ^ (d & 1), :, z1 ^ (d >> 1)]

    piece = jax.ShapeDtypeStruct((2, HALF, HALF), BF16)
    chosen = pl.BlockSpec((1, 2, HALF, STATES), lambda i, pos: (pos[X1] ^ turn, 0, 0, 0))
    return pl.pallas_call(
        kernel,
        grid_spec=pltpu.PrefetchScalarGridSpec(
            num_scalar_prefetch=1,
            grid=(1,),
            in_specs=[chosen, chosen, pl.BlockSpec((1, STATES, 4 * STATES), lambda i, pos: (1, 0, 0))],
            out_specs=[pl.BlockSpec((2, HALF, HALF), lambda i, pos: (0, 0, 0))] * 4,
            scratch_shapes=[
                pltpu.VMEM((2, 2, 2, HALF, HALF), BF16),
                pltpu.VMEM((2 * STATES, 4 * STATES), BF16),
                pltpu.VMEM((2, 2, 2, HALF, HALF), BF16),
            ],
        ),
        out_shape=[piece] * 4,
        compiler_params=pltpu.CompilerParams(vmem_limit_bytes=VMEM),
        cost_estimate=cost(4 * 2**30, 4 * 2**20),
        name="section_1",
    )(pos, kept, arrived, weights)


def third_section(pos, pieces, weights, turn, earlier):
    def kernel(pos_ref, a00, a01, a10, a11, w_ref, *rest):
        o_ref, x_ref, lhs_ref = rest[-3:]
        z1, x0 = pos_ref[Z1], pos_ref[X0]
        for d, a_ref in enumerate((a00, a01, a10, a11)):
            for part in range(2):
                x_ref[x0 ^ (d & 1), part, z1 ^ (d >> 1)] = a_ref[part]

        def emit(tile, value):
            o_ref[:, :, tile * HALF : tile * HALF + HALF] = value.reshape(2, STATES, HALF)

        channel(lambda tile, part: x_ref[tile, part].reshape(STATES, HALF), w_ref, lhs_ref, emit)

    piece = pl.BlockSpec((2, HALF, HALF), lambda i, pos: (0, 0, 0))
    in_specs = [piece] * 4 + [pl.BlockSpec((1, STATES, 4 * STATES), lambda i, pos: (2, 0, 0))]
    args = (pos, *pieces, weights)
    aliases = {}
    if earlier is not None:
        in_specs.append(pl.BlockSpec(memory_space=pl.ANY))
        args = (*args, earlier)
        aliases = {len(args) - 1: 0}
    return pl.pallas_call(
        kernel,
        grid_spec=pltpu.PrefetchScalarGridSpec(
            num_scalar_prefetch=1,
            grid=(1,),
            in_specs=in_specs,
            out_specs=pl.BlockSpec((2, STATES, STATES), lambda i, pos: (0, 0, pos[YHI] ^ turn)),
            scratch_shapes=[
                pltpu.VMEM((2, 2, 2, HALF, HALF), BF16),
                pltpu.VMEM((2 * STATES, 4 * STATES), BF16),
            ],
        ),
        out_shape=jax.ShapeDtypeStruct((2, STATES, 2 * STATES), BF16),
        input_output_aliases=aliases,
        compiler_params=pltpu.CompilerParams(vmem_limit_bytes=VMEM),
        cost_estimate=cost(4 * 2**30, 4 * 2**20),
        name="section_2",
    )(*args)


def route(d1, d2, d3):
    pairs = []
    for device in range(128):
        ylo, z1, z0, core, x1, x0, yhi = (device >> place & 1 for place in range(6, -1, -1))
        goal = 0
        for bit in (z0, z1 ^ d1, core, ylo, yhi, x0 ^ d2, x1 ^ d3):
            goal = goal * 2 + bit
        pairs.append((device, goal))
    return pairs


def body(density, kraus, targets):
    pos = jnp.stack([lax.axis_index(name) for name in ("core", "x1", "z1", "x0", "yhi")]).astype(jnp.int32)
    packed = pack(density).reshape(32, 2, 64, 256)
    arrived = lax.all_to_all(packed, GATHERED, split_axis=0, concat_axis=0, tiled=True)
    weights = operators(kraus, targets)
    kept, sent = first_section(pos, arrived.reshape(8, 4, 2, 64, 256), weights)
    swapped = lax.ppermute(sent, "core", [(0, 1), (1, 0)])
    landed = []
    for turn in range(2):
        pieces = second_section(pos, kept, swapped, weights, turn)
        landed.append([lax.ppermute(piece, AXES, route(d >> 1, d & 1, turn)) for d, piece in enumerate(pieces)])
    out = None
    for turn in range(2):
        out = third_section(pos, landed[turn], weights, turn, out)
    return out


def solution(mesh):
    fine = Mesh(mesh.devices.reshape((2,) * len(AXES)), AXES)
    split = P(None, AXES[:4], AXES[4:])
    return jax.shard_map(body, mesh=fine, in_specs=(split, P(), P()), out_specs=split, check_vma=False)
```

```python
import itertools

import jax
import jax.numpy as jnp
from jax import lax
from jax.experimental import pallas as pl
from jax.experimental.pallas import tpu as pltpu
from jax.sharding import Mesh
from jax.sharding import PartitionSpec as P

STATES = 512
QUBITS = 9
SECTIONS = 3
HALF = 256
BF16 = jnp.bfloat16
F32 = jnp.float32
AXES = ("ylo", "z1", "z0", "core", "x1", "x0", "yhi")
GATHERED = ("z1", "z0", "core", "x0", "yhi")
CORE, X1, Z1, X0, Z0, YLO = range(6)
VMEM = 48 * 2**20


def cost(flops, data):
    return pl.CostEstimate(flops=flops, bytes_accessed=data, transcendentals=0)


def pack(pos, density):
    def kernel(pos_ref, x_ref, o_ref):
        for b7, b6, low, high, top in itertools.product(range(2), repeat=5):
            rows = (b7 * 2 + b6) * 64
            lanes = (top * 4 + high * 2 + low) * 128
            o_ref[b7, low, b6, high, 0, :, :, top * 128 : top * 128 + 128] = x_ref[:, rows : rows + 64, lanes : lanes + 128]

    return pl.pallas_call(
        kernel,
        grid_spec=pltpu.PrefetchScalarGridSpec(
            num_scalar_prefetch=1,
            grid=(2,),
            in_specs=[pl.BlockSpec((2, HALF, 1024), lambda b8, pos: (0, b8, 0))],
            out_specs=pl.BlockSpec(
                (2, 2, 2, 2, 1, 2, 64, 256), lambda b8, pos: (0, 0, 0, 0, b8 ^ pos[YLO], 0, 0, 0)
            ),
        ),
        out_shape=jax.ShapeDtypeStruct((2, 2, 2, 2, 2, 2, 64, 256), BF16),
        cost_estimate=cost(0, 2**22),
        name="pack",
    )(pos, density)


def operators(kraus, targets):
    def kernel(t_ref, k_ref, o_ref):
        section = pl.program_id(0)

        def order(state):
            total = jnp.zeros_like(state)
            for bit in range(QUBITS):
                total += ((state >> t_ref[section, bit]) & 1) << bit
            return total

        out_state = lax.broadcasted_iota(jnp.int32, (STATES, 1), 0)
        place = lax.broadcasted_iota(jnp.int32, (1, STATES), 1)
        mixed = ((place >> 5 & 1) << 8) | ((place >> 6 & 7) << 5) | (place & 31)
        in_state = jnp.where(section == 0, mixed, place)
        lanes = lax.broadcasted_iota(jnp.int32, (STATES, STATES), 1)
        rows = lax.broadcasted_iota(jnp.int32, (STATES, STATES), 0)
        left = (order(out_state) == lanes).astype(F32).astype(BF16)
        right = (order(in_state) == rows).astype(F32).astype(BF16)
        for term in range(2):
            for part in range(2):
                picked = jnp.dot(left, k_ref[0, term, part], preferred_element_type=F32).astype(BF16)
                at = (term * 2 + part) * STATES
                o_ref[0, :, at : at + STATES] = jnp.dot(picked, right, preferred_element_type=F32).astype(BF16)

    return pl.pallas_call(
        kernel,
        grid=(SECTIONS,),
        in_specs=[
            pl.BlockSpec(memory_space=pltpu.SMEM),
            pl.BlockSpec((1, 2, 2, STATES, STATES), lambda s: (s, 0, 0, 0, 0)),
        ],
        out_specs=pl.BlockSpec((1, STATES, 4 * STATES), lambda s: (s, 0, 0)),
        out_shape=jax.ShapeDtypeStruct((SECTIONS, STATES, 4 * STATES), BF16),
        compiler_params=pltpu.CompilerParams(vmem_limit_bytes=VMEM),
        cost_estimate=cost(24 * 2 * 512**3, 12 * 2**20),
        name="operators",
    )(targets, kraus)


def channel(x, w_ref, lhs_ref, emit):
    for tile in range(2):
        for part in range(2):
            if part == 0:
                columns = jnp.concatenate([x(tile, 0), -x(tile, 1)], axis=0)
            else:
                columns = jnp.concatenate([x(tile, 1), x(tile, 0)], axis=0)
            for term in range(2):
                product = jnp.dot(
                    w_ref[0, :, term * 1024 : term * 1024 + 1024], columns, preferred_element_type=F32
                ).astype(BF16)
                at = term * 1024 + part * STATES + tile * HALF
                lhs_ref[0:STATES, at : at + HALF] = product
                other = term * 1024 + (1 - part) * STATES + tile * HALF
                lhs_ref[STATES:, other : other + HALF] = product if part else -product
    for tile in range(2):
        total = lax.dot_general(
            lhs_ref[...],
            w_ref[0, tile * HALF : tile * HALF + HALF, :],
            (((1,), (1,)), ((), ())),
            preferred_element_type=F32,
        )
        emit(tile, total.astype(BF16))


def first_section(pos, arrived, weights):
    def kernel(pos_ref, a_ref, w_ref, keep_ref, send_ref, x_ref, lhs_ref, out_ref):
        step = pl.program_id(0)

        @pl.when(step == 0)
        def _():
            for source in range(8):
                for col in range(4):
                    for part in range(2):
                        low = a_ref[source, col, part, :, 0:128]
                        high = a_ref[source, col, part, :, 128:256]
                        rows = slice(source * 64, source * 64 + 64)
                        lanes = slice((col & 1) * 128, (col & 1) * 128 + 128)
                        x_ref[0, col >> 1, part, rows, lanes] = jnp.concatenate([low[:, :64], high[:, :64]], axis=1)
                        x_ref[1, col >> 1, part, rows, lanes] = jnp.concatenate([low[:, 64:], high[:, 64:]], axis=1)

        core = pos_ref[CORE]

        def emit(tile, value):
            out_ref[tile] = value.reshape(2, 2, HALF, HALF)

        channel(lambda tile, part: x_ref[step, tile, part], w_ref, lhs_ref, emit)
        for low in range(2):
            for part in range(2):
                keep_ref[low, part] = out_ref[core, part, low]
                send_ref[low, part] = out_ref[1 - core, part, low]

    half = jax.ShapeDtypeStruct((2, 2, HALF, STATES), BF16)
    return pl.pallas_call(
        kernel,
        grid_spec=pltpu.PrefetchScalarGridSpec(
            num_scalar_prefetch=1,
            grid=(2,),
            in_specs=[
                pl.BlockSpec((8, 4, 2, 64, 256), lambda h, pos: (0, 0, 0, 0, 0)),
                pl.BlockSpec((1, STATES, 4 * STATES), lambda h, pos: (0, 0, 0)),
            ],
            out_specs=[pl.BlockSpec((2, 2, HALF, HALF), lambda h, pos: (0, 0, 0, h))] * 2,
            scratch_shapes=[
                pltpu.VMEM((2, 2, 2, STATES, HALF), BF16),
                pltpu.VMEM((2 * STATES, 4 * STATES), BF16),
                pltpu.VMEM((2, 2, 2, HALF, HALF), BF16),
            ],
        ),
        out_shape=[half, half],
        compiler_params=pltpu.CompilerParams(vmem_limit_bytes=VMEM),
        cost_estimate=cost(8 * 2**30, 6 * 2**20),
        name="section_0",
    )(pos, arrived, weights)


def second_section(pos, kept, arrived, weights, turn):
    def kernel(pos_ref, k_ref, a_ref, w_ref, o00, o01, o10, o11, x_ref, lhs_ref, out_ref):
        core, z1, x1 = pos_ref[CORE], pos_ref[Z1], pos_ref[X1]
        for tile in range(2):
            for part in range(2):
                lanes = slice(tile * HALF, tile * HALF + HALF)
                x_ref[tile, part, core] = k_ref[0, part, :, lanes]
                x_ref[tile, part, 1 - core] = a_ref[0, part, :, lanes]

        def emit(tile, value):
            out_ref[tile] = value.reshape(2, 2, HALF, HALF)

        channel(lambda tile, part: x_ref[tile, part].reshape(STATES, HALF), w_ref, lhs_ref, emit)
        for d, o_ref in enumerate((o00, o01, o10, o11)):
            o_ref[...] = out_ref[x1 ^ (d & 1), :, z1 ^ (d >> 1)]

    piece = jax.ShapeDtypeStruct((2, HALF, HALF), BF16)
    chosen = pl.BlockSpec((1, 2, HALF, STATES), lambda i, pos: (pos[Z0] ^ turn, 0, 0, 0))
    return pl.pallas_call(
        kernel,
        grid_spec=pltpu.PrefetchScalarGridSpec(
            num_scalar_prefetch=1,
            grid=(1,),
            in_specs=[chosen, chosen, pl.BlockSpec((1, STATES, 4 * STATES), lambda i, pos: (1, 0, 0))],
            out_specs=[pl.BlockSpec((2, HALF, HALF), lambda i, pos: (0, 0, 0))] * 4,
            scratch_shapes=[
                pltpu.VMEM((2, 2, 2, HALF, HALF), BF16),
                pltpu.VMEM((2 * STATES, 4 * STATES), BF16),
                pltpu.VMEM((2, 2, 2, HALF, HALF), BF16),
            ],
        ),
        out_shape=[piece] * 4,
        compiler_params=pltpu.CompilerParams(vmem_limit_bytes=VMEM),
        cost_estimate=cost(4 * 2**30, 4 * 2**20),
        name="section_1",
    )(pos, kept, arrived, weights)


def third_section(pos, pieces, weights, turn, earlier):
    def kernel(pos_ref, a00, a01, a10, a11, w_ref, *rest):
        o_ref, x_ref, lhs_ref = rest[-3:]
        z1, z0 = pos_ref[Z1], pos_ref[Z0]
        for d, a_ref in enumerate((a00, a01, a10, a11)):
            for part in range(2):
                x_ref[z0 ^ (d & 1), part, z1 ^ (d >> 1)] = a_ref[part]

        def emit(tile, value):
            o_ref[:, :, tile * HALF : tile * HALF + HALF] = value.reshape(2, STATES, HALF)

        channel(lambda tile, part: x_ref[tile, part].reshape(STATES, HALF), w_ref, lhs_ref, emit)

    piece = pl.BlockSpec((2, HALF, HALF), lambda i, pos: (0, 0, 0))
    in_specs = [piece] * 4 + [pl.BlockSpec((1, STATES, 4 * STATES), lambda i, pos: (2, 0, 0))]
    args = (pos, *pieces, weights)
    aliases = {}
    if earlier is not None:
        in_specs.append(pl.BlockSpec(memory_space=pl.ANY))
        args = (*args, earlier)
        aliases = {len(args) - 1: 0}
    return pl.pallas_call(
        kernel,
        grid_spec=pltpu.PrefetchScalarGridSpec(
            num_scalar_prefetch=1,
            grid=(1,),
            in_specs=in_specs,
            out_specs=pl.BlockSpec((2, STATES, STATES), lambda i, pos: (0, 0, pos[X0] ^ turn)),
            scratch_shapes=[
                pltpu.VMEM((2, 2, 2, HALF, HALF), BF16),
                pltpu.VMEM((2 * STATES, 4 * STATES), BF16),
            ],
        ),
        out_shape=jax.ShapeDtypeStruct((2, STATES, 2 * STATES), BF16),
        input_output_aliases=aliases,
        compiler_params=pltpu.CompilerParams(vmem_limit_bytes=VMEM),
        cost_estimate=cost(4 * 2**30, 4 * 2**20),
        name="section_2",
    )(*args)


def route(d1, d2, d3):
    pairs = []
    for device in range(128):
        ylo, z1, z0, core, x1, x0, yhi = (device >> place & 1 for place in range(6, -1, -1))
        goal = 0
        for bit in (yhi ^ ylo, z1 ^ d1, z0 ^ d3, ylo, x0, x1 ^ d2, core):
            goal = goal * 2 + bit
        pairs.append((device, goal))
    return pairs


def body(density, kraus, targets):
    pos = jnp.stack([lax.axis_index(name) for name in ("core", "x1", "z1", "x0", "z0", "ylo")]).astype(jnp.int32)
    packed = pack(pos, density).reshape(32, 2, 64, 256)
    arrived = lax.all_to_all(packed, GATHERED, split_axis=0, concat_axis=0, tiled=True)
    weights = operators(kraus, targets)
    kept, sent = first_section(pos, arrived.reshape(8, 4, 2, 64, 256), weights)
    swapped = lax.ppermute(sent, "core", [(0, 1), (1, 0)])
    landed = {}
    for d3 in range(2):
        pieces = second_section(pos, kept, swapped, weights, d3)
        for d2, d1 in itertools.product(range(2), repeat=2):
            landed[d1, d2, d3] = lax.ppermute(pieces[d1 * 2 + d2], AXES, route(d1, d2, d3))
    out = None
    for d2 in range(2):
        pieces = [landed[d1, d2, d3] for d1, d3 in itertools.product(range(2), repeat=2)]
        out = third_section(pos, pieces, weights, d2, out)
    return out


def solution(mesh):
    fine = Mesh(mesh.devices.reshape((2,) * len(AXES)), AXES)
    split = P(None, AXES[:4], AXES[4:])
    return jax.shard_map(body, mesh=fine, in_specs=(split, P(), P()), out_specs=split, check_vma=False)
```

```python
import itertools

import jax
import jax.numpy as jnp
from jax import lax
from jax.experimental import pallas as pl
from jax.experimental.pallas import tpu as pltpu
from jax.sharding import Mesh
from jax.sharding import PartitionSpec as P

STATES = 512
QUBITS = 9
SECTIONS = 3
HALF = 256
BF16 = jnp.bfloat16
F32 = jnp.float32
AXES = ("ylo", "z1", "z0", "core", "x1", "x0", "yhi")
GATHERED = ("z1", "z0", "core", "x0", "yhi")
VMEM = 20 * 2**20
IN_VMEM = pl.BlockSpec(memory_space=pltpu.VMEM)
IN_HBM = pl.BlockSpec(memory_space=pltpu.HBM)


def cost(flops, data):
    return pl.CostEstimate(flops=flops, bytes_accessed=data, transcendentals=0)


LIGHT = cost(2**26, 2**16)


def pack(density):
    def kernel(x_ref, o_ref):
        ylo = lax.axis_index("ylo")
        for b8, b7, b6, low, high, top in itertools.product(range(2), repeat=6):
            rows = (b8 * 4 + b7 * 2 + b6) * 64
            lanes = (top * 4 + high * 2 + low) * 128
            tile = x_ref[:, rows : rows + 64, lanes : lanes + 128]
            o_ref[b7, low, b6, high, b8 ^ ylo, :, :, top * 128 : top * 128 + 128] = tile

    return pl.pallas_call(
        kernel,
        in_specs=[IN_VMEM],
        out_specs=IN_VMEM,
        out_shape=jax.ShapeDtypeStruct((2, 2, 2, 2, 2, 2, 64, 256), BF16),
        compiler_params=pltpu.CompilerParams(vmem_limit_bytes=VMEM),
        cost_estimate=cost(0, 2**22),
        name="pack",
    )(density)


def operators(kraus, targets, section):
    def kernel(t_ref, k_ref, o_ref):
        def order(state):
            total = jnp.zeros_like(state)
            for bit in range(QUBITS):
                total += ((state >> t_ref[section, bit]) & 1) << bit
            return total

        out_state = lax.broadcasted_iota(jnp.int32, (STATES, 1), 0)
        in_state = lax.broadcasted_iota(jnp.int32, (1, STATES), 1)
        if section == 0:
            in_state = ((in_state >> 5 & 1) << 8) | ((in_state >> 6 & 7) << 5) | (in_state & 31)
        lanes = lax.broadcasted_iota(jnp.int32, (STATES, STATES), 1)
        rows = lax.broadcasted_iota(jnp.int32, (STATES, STATES), 0)
        left = (order(out_state) == lanes).astype(F32).astype(BF16)
        right = (order(in_state) == rows).astype(F32).astype(BF16)
        for part in range(2):
            picked = jnp.dot(left, k_ref[0, 0, part], preferred_element_type=F32).astype(BF16)
            at = part * STATES
            o_ref[0, :, at : at + STATES] = jnp.dot(picked, right, preferred_element_type=F32).astype(BF16)

    return pl.pallas_call(
        kernel,
        grid=(2,),
        in_specs=[
            pl.BlockSpec(memory_space=pltpu.SMEM),
            pl.BlockSpec((1, 1, 2, STATES, STATES), lambda term: (section, term, 0, 0, 0)),
        ],
        out_specs=pl.BlockSpec((1, STATES, 2 * STATES), lambda term: (term, 0, 0)),
        out_shape=jax.ShapeDtypeStruct((2, STATES, 2 * STATES), BF16),
        compiler_params=pltpu.CompilerParams(vmem_limit_bytes=54 * 2**20),
        cost_estimate=cost(8 * 2 * 512**3, 4 * 2**20),
        name="operators",
    )(targets, kraus)


def left(x, w_ref, lhs_ref, first=0, rows=STATES):
    for tile in range(2):
        for part in range(2):
            if part == 0:
                columns = jnp.concatenate([x(tile, 0), -x(tile, 1)], axis=0)
            else:
                columns = jnp.concatenate([x(tile, 1), x(tile, 0)], axis=0)
            products = jnp.dot(
                w_ref[:, pl.ds(first, rows)].reshape(2 * rows, 2 * STATES), columns, preferred_element_type=F32
            ).astype(BF16)
            for term in range(2):
                product = products[term * rows : term * rows + rows]
                at = term * 1024 + part * STATES + tile * HALF
                lhs_ref[0:rows, at : at + HALF] = product
                other = term * 1024 + (1 - part) * STATES + tile * HALF
                lhs_ref[rows:, other : other + HALF] = product if part else -product


def right(lhs, w_ref, emit):
    for tile in range(2):
        total = lax.dot_general(
            lhs[...],
            jnp.concatenate([w_ref[term, tile * HALF : tile * HALF + HALF] for term in range(2)], axis=1),
            (((1,), (1,)), ((), ())),
            preferred_element_type=F32,
        )
        emit(tile, total.astype(BF16))


def first_section(arrived, weights):
    def kernel(a_ref, w_ref, keep_ref, send_ref, x_ref, lhs_ref, out_ref):
        core = lax.axis_index("core")
        for source, col, part in itertools.product(range(8), range(4), range(2)):
            low = a_ref[source, col, part, :, 0:128]
            high = a_ref[source, col, part, :, 128:256]
            rows = slice(source * 64, source * 64 + 64)
            lanes = slice((col & 1) * 128, (col & 1) * 128 + 128)
            x_ref[0, col >> 1, part, rows, lanes] = jnp.concatenate([low[:, :64], high[:, :64]], axis=1)
            x_ref[1, col >> 1, part, rows, lanes] = jnp.concatenate([low[:, 64:], high[:, 64:]], axis=1)

        @pl.loop(0, 2)
        def _(step):
            def emit(tile, value):
                out_ref[tile] = value.reshape(2, 2, HALF, HALF)

            left(lambda tile, part: x_ref[step, tile, part], w_ref, lhs_ref)
            right(lhs_ref, w_ref, emit)
            for low, part in itertools.product(range(2), repeat=2):
                keep_ref[low, part, step] = out_ref[core, part, low]
                send_ref[low, part, step] = out_ref[1 - core, part, low]

    half = jax.ShapeDtypeStruct((2, 2, 2, HALF, HALF), BF16)
    return pl.pallas_call(
        kernel,
        in_specs=[IN_VMEM] * 2,
        out_specs=[IN_VMEM] * 2,
        scratch_shapes=[
            pltpu.VMEM((2, 2, 2, STATES, HALF), BF16),
            pltpu.VMEM((2 * STATES, 4 * STATES), BF16),
            pltpu.VMEM((2, 2, 2, HALF, HALF), BF16),
        ],
        out_shape=[half, half],
        compiler_params=pltpu.CompilerParams(vmem_limit_bytes=VMEM),
        cost_estimate=LIGHT,
        name="section_0",
    )(arrived, weights)


def second_section(kept, arrived, weights, turn):
    def kernel(k_ref, a_ref, w_ref, o00, o01, o10, o11, x_ref, lhs_ref, out_ref):
        core, z1, x1 = lax.axis_index("core"), lax.axis_index("z1"), lax.axis_index("x1")
        low = lax.axis_index("z0") ^ turn
        for tile, part in itertools.product(range(2), repeat=2):
            x_ref[tile, part, core] = k_ref[low, part, tile]
            x_ref[tile, part, 1 - core] = a_ref[low, part, tile]

        def emit(tile, value):
            out_ref[tile] = value.reshape(2, 2, HALF, HALF)

        left(lambda tile, part: x_ref[tile, part].reshape(STATES, HALF), w_ref, lhs_ref)
        right(lhs_ref, w_ref, emit)
        for d, o_ref in enumerate((o00, o01, o10, o11)):
            o_ref[...] = out_ref[x1 ^ (d & 1), :, z1 ^ (d >> 1)]

    piece = jax.ShapeDtypeStruct((2, HALF, HALF), BF16)
    return pl.pallas_call(
        kernel,
        in_specs=[IN_VMEM] * 3,
        out_specs=[IN_VMEM] * 4,
        scratch_shapes=[
            pltpu.VMEM((2, 2, 2, HALF, HALF), BF16),
            pltpu.VMEM((2 * STATES, 4 * STATES), BF16),
            pltpu.VMEM((2, 2, 2, HALF, HALF), BF16),
        ],
        out_shape=[piece] * 4,
        compiler_params=pltpu.CompilerParams(vmem_limit_bytes=VMEM),
        cost_estimate=LIGHT,
        name="section_1",
    )(kept, arrived, weights)


def third_section(pieces, weights, turn, earlier):
    def kernel(a00, a01, a10, a11, w_ref, *rest):
        o_ref, x_ref, lhs_ref, out_ref, sem = rest[-5:]
        z1, z0 = lax.axis_index("z1"), lax.axis_index("z0")
        first = (lax.axis_index("x0") ^ turn) * STATES
        for d, a_ref in enumerate((a00, a01, a10, a11)):
            for part in range(2):
                x_ref[z0 ^ (d & 1), part, z1 ^ (d >> 1)] = a_ref[part]
        writes = []

        def emit(tile, value):
            out_ref[tile] = value.reshape(2, STATES, HALF)
            lanes = pl.ds(pl.multiple_of(first + tile * HALF, HALF), HALF)
            writes.append(pltpu.make_async_copy(out_ref.at[tile], o_ref.at[:, :, lanes], sem.at[tile]))
            writes[-1].start()

        left(lambda tile, part: x_ref[tile, part].reshape(STATES, HALF), w_ref, lhs_ref)
        right(lhs_ref, w_ref, emit)
        for write in writes:
            write.wait()

    in_specs = [IN_VMEM] * 5
    args = (*pieces, weights)
    aliases = {}
    if earlier is not None:
        in_specs.append(IN_HBM)
        args = (*args, earlier)
        aliases = {len(args) - 1: 0}
    return pl.pallas_call(
        kernel,
        in_specs=in_specs,
        out_specs=IN_HBM,
        scratch_shapes=[
            pltpu.VMEM((2, 2, 2, HALF, HALF), BF16),
            pltpu.VMEM((2 * STATES, 4 * STATES), BF16),
            pltpu.VMEM((2, 2, STATES, HALF), BF16),
            pltpu.SemaphoreType.DMA((2,)),
        ],
        out_shape=jax.ShapeDtypeStruct((2, STATES, 2 * STATES), BF16),
        input_output_aliases=aliases,
        compiler_params=pltpu.CompilerParams(vmem_limit_bytes=VMEM),
        cost_estimate=LIGHT,
        name="section_2",
    )(*args)


def route(d1, d2, d3):
    pairs = []
    for device in range(128):
        ylo, z1, z0, core, x1, x0, yhi = (device >> place & 1 for place in range(6, -1, -1))
        goal = 0
        for bit in (yhi ^ ylo, z1 ^ d1, z0 ^ d3, ylo, x0, x1 ^ d2, core):
            goal = goal * 2 + bit
        pairs.append((device, goal))
    return pairs


def body(density, kraus, targets):
    packed = pack(density).reshape(32, 2, 64, 256)
    arrived = lax.all_to_all(packed, GATHERED, split_axis=0, concat_axis=0, tiled=True)
    arrived = arrived.reshape(8, 4, 2, 64, 256)
    weights = [operators(kraus, targets, section) for section in range(SECTIONS)]
    weights = list(lax.optimization_barrier(weights))
    kept, sent = first_section(arrived, weights[0])
    swapped = lax.ppermute(sent, "core", [(0, 1), (1, 0)])
    landed = {}
    for d3 in range(2):
        pieces = second_section(kept, swapped, weights[1], d3)
        for d2, d1 in itertools.product(range(2), repeat=2):
            landed[d1, d2, d3] = lax.ppermute(pieces[d1 * 2 + d2], AXES, route(d1, d2, d3))
    out = None
    for d2 in range(2):
        pieces = [landed[d1, d2, d3] for d1, d3 in itertools.product(range(2), repeat=2)]
        out = third_section(pieces, weights[2], d2, out)
    return out


def solution(mesh):
    fine = Mesh(mesh.devices.reshape((2,) * len(AXES)), AXES)
    split = P(None, AXES[:4], AXES[4:])
    return jax.shard_map(body, mesh=fine, in_specs=(split, P(), P()), out_specs=split, check_vma=False)
```

```python
import itertools

import jax
import jax.numpy as jnp
from jax import lax
from jax.experimental import pallas as pl
from jax.experimental.pallas import tpu as pltpu
from jax.sharding import Mesh
from jax.sharding import PartitionSpec as P

STATES = 512
QUBITS = 9
SECTIONS = 3
HALF = 256
BF16 = jnp.bfloat16
F32 = jnp.float32
AXES = ("ylo", "z1", "z0", "core", "x1", "x0", "yhi")
GATHERED = ("z1", "z0", "core", "x0", "yhi")
VMEM = 20 * 2**20
IN_VMEM = pl.BlockSpec(memory_space=pltpu.VMEM)
IN_HBM = pl.BlockSpec(memory_space=pltpu.HBM)


def cost(flops, data):
    return pl.CostEstimate(flops=flops, bytes_accessed=data, transcendentals=0)


LIGHT = cost(2**26, 2**16)


def pack(density):
    def kernel(x_ref, o_ref, in_ref, out_ref, sem):
        ylo = lax.axis_index("ylo")
        reads, writes = [], []
        for step in range(4):
            rows = pl.ds(step * 128, 128)
            reads.append(pltpu.make_async_copy(x_ref.at[:, rows], in_ref.at[step], sem.at[0, step]))
            reads[-1].start()
        for step in range(4):
            b8, b7 = step >> 1, step & 1
            reads[step].wait()
            for b6, low, high, top in itertools.product(range(2), repeat=4):
                lanes = (top * 4 + high * 2 + low) * 128
                tile = in_ref[step, :, b6 * 64 : b6 * 64 + 64, lanes : lanes + 128]
                out_ref[step, low, b6, high, :, :, top * 128 : top * 128 + 128] = tile
            writes.append(pltpu.make_async_copy(out_ref.at[step], o_ref.at[b7, :, :, :, b8 ^ ylo], sem.at[1, step]))
            writes[-1].start()
        for write in writes:
            write.wait()

    return pl.pallas_call(
        kernel,
        in_specs=[IN_HBM],
        out_specs=IN_HBM,
        out_shape=jax.ShapeDtypeStruct((2, 2, 2, 2, 2, 2, 64, 256), BF16),
        scratch_shapes=[
            pltpu.VMEM((4, 2, 128, 1024), BF16),
            pltpu.VMEM((4, 2, 2, 2, 2, 64, 256), BF16),
            pltpu.SemaphoreType.DMA((2, 4)),
        ],
        compiler_params=pltpu.CompilerParams(vmem_limit_bytes=62 * 2**20),
        cost_estimate=cost(0, 2**22),
        name="pack",
    )(density)


def operators(kraus, targets, section):
    def kernel(t_ref, k_ref, o_ref):
        def order(state):
            total = jnp.zeros_like(state)
            for bit in range(QUBITS):
                total += ((state >> t_ref[section, bit]) & 1) << bit
            return total

        out_state = lax.broadcasted_iota(jnp.int32, (STATES, 1), 0)
        in_state = lax.broadcasted_iota(jnp.int32, (1, STATES), 1)
        if section == 0:
            in_state = ((in_state >> 5 & 1) << 8) | ((in_state >> 6 & 7) << 5) | (in_state & 31)
        lanes = lax.broadcasted_iota(jnp.int32, (STATES, STATES), 1)
        rows = lax.broadcasted_iota(jnp.int32, (STATES, STATES), 0)
        left = (order(out_state) == lanes).astype(F32).astype(BF16)
        right = (order(in_state) == rows).astype(F32).astype(BF16)
        for part in range(2):
            picked = jnp.dot(left, k_ref[0, 0, part], preferred_element_type=F32).astype(BF16)
            at = part * STATES
            o_ref[0, :, at : at + STATES] = jnp.dot(picked, right, preferred_element_type=F32).astype(BF16)

    return pl.pallas_call(
        kernel,
        grid=(2,),
        in_specs=[
            pl.BlockSpec(memory_space=pltpu.SMEM),
            pl.BlockSpec((1, 1, 2, STATES, STATES), lambda term: (section, term, 0, 0, 0)),
        ],
        out_specs=pl.BlockSpec((1, STATES, 2 * STATES), lambda term: (term, 0, 0)),
        out_shape=jax.ShapeDtypeStruct((2, STATES, 2 * STATES), BF16),
        compiler_params=pltpu.CompilerParams(vmem_limit_bytes=54 * 2**20),
        cost_estimate=cost(8 * 2 * 512**3, 4 * 2**20),
        name="operators",
    )(targets, kraus)


def left(x, w_ref, lhs_ref, first=0, rows=STATES):
    for tile in range(2):
        for part in range(2):
            if part == 0:
                columns = jnp.concatenate([x(tile, 0), -x(tile, 1)], axis=0)
            else:
                columns = jnp.concatenate([x(tile, 1), x(tile, 0)], axis=0)
            products = jnp.dot(
                w_ref[:, pl.ds(first, rows)].reshape(2 * rows, 2 * STATES), columns, preferred_element_type=F32
            ).astype(BF16)
            for term in range(2):
                product = products[term * rows : term * rows + rows]
                at = term * 1024 + part * STATES + tile * HALF
                lhs_ref[0:rows, at : at + HALF] = product
                other = term * 1024 + (1 - part) * STATES + tile * HALF
                lhs_ref[rows:, other : other + HALF] = product if part else -product


def right(lhs, w_ref, emit):
    for tile in range(2):
        total = lax.dot_general(
            lhs[...],
            jnp.concatenate([w_ref[term, tile * HALF : tile * HALF + HALF] for term in range(2)], axis=1),
            (((1,), (1,)), ((), ())),
            preferred_element_type=F32,
        )
        emit(tile, total.astype(BF16))


def first_section(arrived, weights):
    def kernel(a_hbm, w_ref, keep_ref, send_ref, a_ref, x_ref, lhs_ref, out_ref, sem):
        core = lax.axis_index("core")
        reads = [pltpu.make_async_copy(a_hbm.at[:, col], a_ref.at[col], sem.at[col]) for col in range(4)]
        for read in reads:
            read.start()
        for col, read in enumerate(reads):
            read.wait()
            for source, part in itertools.product(range(8), range(2)):
                low = a_ref[col, source, part, :, 0:128]
                high = a_ref[col, source, part, :, 128:256]
                rows = slice(source * 64, source * 64 + 64)
                lanes = slice((col & 1) * 128, (col & 1) * 128 + 128)
                x_ref[0, col >> 1, part, rows, lanes] = jnp.concatenate([low[:, :64], high[:, :64]], axis=1)
                x_ref[1, col >> 1, part, rows, lanes] = jnp.concatenate([low[:, 64:], high[:, 64:]], axis=1)

        @pl.loop(0, 2)
        def _(step):
            def emit(tile, value):
                out_ref[tile] = value.reshape(2, 2, HALF, HALF)

            left(lambda tile, part: x_ref[step, tile, part], w_ref, lhs_ref)
            right(lhs_ref, w_ref, emit)
            for low, part in itertools.product(range(2), repeat=2):
                keep_ref[low, part, step] = out_ref[core, part, low]
                send_ref[low, part, step] = out_ref[1 - core, part, low]

    half = jax.ShapeDtypeStruct((2, 2, 2, HALF, HALF), BF16)
    return pl.pallas_call(
        kernel,
        in_specs=[IN_HBM, IN_VMEM],
        out_specs=[IN_VMEM] * 2,
        scratch_shapes=[
            pltpu.VMEM((4, 8, 2, 64, 256), BF16),
            pltpu.VMEM((2, 2, 2, STATES, HALF), BF16),
            pltpu.VMEM((2 * STATES, 4 * STATES), BF16),
            pltpu.VMEM((2, 2, 2, HALF, HALF), BF16),
            pltpu.SemaphoreType.DMA((4,)),
        ],
        out_shape=[half, half],
        compiler_params=pltpu.CompilerParams(vmem_limit_bytes=VMEM),
        cost_estimate=LIGHT,
        name="section_0",
    )(arrived, weights)


def second_section(kept, arrived, weights, turn):
    def kernel(k_ref, a_ref, w_ref, o00, o01, o10, o11, x_ref, lhs_ref, out_ref):
        core, z1, x1 = lax.axis_index("core"), lax.axis_index("z1"), lax.axis_index("x1")
        low = lax.axis_index("z0") ^ turn
        for tile, part in itertools.product(range(2), repeat=2):
            x_ref[tile, part, core] = k_ref[low, part, tile]
            x_ref[tile, part, 1 - core] = a_ref[low, part, tile]

        def emit(tile, value):
            out_ref[tile] = value.reshape(2, 2, HALF, HALF)

        left(lambda tile, part: x_ref[tile, part].reshape(STATES, HALF), w_ref, lhs_ref)
        right(lhs_ref, w_ref, emit)
        for d, o_ref in enumerate((o00, o01, o10, o11)):
            o_ref[...] = out_ref[x1 ^ (d & 1), :, z1 ^ (d >> 1)]

    piece = jax.ShapeDtypeStruct((2, HALF, HALF), BF16)
    return pl.pallas_call(
        kernel,
        in_specs=[IN_VMEM] * 3,
        out_specs=[IN_VMEM] * 4,
        scratch_shapes=[
            pltpu.VMEM((2, 2, 2, HALF, HALF), BF16),
            pltpu.VMEM((2 * STATES, 4 * STATES), BF16),
            pltpu.VMEM((2, 2, 2, HALF, HALF), BF16),
        ],
        out_shape=[piece] * 4,
        compiler_params=pltpu.CompilerParams(vmem_limit_bytes=VMEM),
        cost_estimate=LIGHT,
        name="section_1",
    )(kept, arrived, weights)


def third_section(pieces, weights):
    def kernel(a00, a01, a10, a11, w_ref, o_ref, x_ref, lhs_ref, out_ref, sem):
        z1, z0 = lax.axis_index("z1"), lax.axis_index("z0")
        first = lax.axis_index("x0") * STATES
        for d, a_ref in enumerate((a00, a01, a10, a11)):
            for part in range(2):
                x_ref[z0 ^ (d & 1), part, z1 ^ (d >> 1)] = a_ref[part]
        writes = []

        def emit(tile, value):
            out_ref[tile] = value.reshape(2, STATES, HALF)
            lanes = pl.ds(pl.multiple_of(first + tile * HALF, HALF), HALF)
            writes.append(pltpu.make_async_copy(out_ref.at[tile], o_ref.at[:, :, lanes], sem.at[tile]))
            writes[-1].start()

        left(lambda tile, part: x_ref[tile, part].reshape(STATES, HALF), w_ref, lhs_ref)
        right(lhs_ref, w_ref, emit)
        for write in writes:
            write.wait()

    return pl.pallas_call(
        kernel,
        in_specs=[IN_VMEM] * 5,
        out_specs=IN_HBM,
        scratch_shapes=[
            pltpu.VMEM((2, 2, 2, HALF, HALF), BF16),
            pltpu.VMEM((2 * STATES, 4 * STATES), BF16),
            pltpu.VMEM((2, 2, STATES, HALF), BF16),
            pltpu.SemaphoreType.DMA((2,)),
        ],
        out_shape=jax.ShapeDtypeStruct((2, STATES, 2 * STATES), BF16),
        compiler_params=pltpu.CompilerParams(vmem_limit_bytes=VMEM),
        cost_estimate=LIGHT,
        name="section_2",
    )(*pieces, weights)


def third_section_half(pieces, weights, turn, partial, earlier):
    def kernel(a0, a1, w_ref, *rest):
        z1, tile = lax.axis_index("z1"), lax.axis_index("z0") ^ turn
        if partial is None:
            o_ref, x_ref, lhs_ref = rest
        else:
            p_ref, _, o_ref, x_ref, lhs_ref, out_ref, sem = rest
        for d, a_ref in enumerate((a0, a1)):
            for part in range(2):
                x_ref[part, z1 ^ d] = a_ref[part]
        real, imag = (x_ref[part].reshape(STATES, HALF) for part in range(2))
        for part in range(2):
            columns = jnp.concatenate([imag, real] if part else [real, -imag], axis=0)
            products = jnp.dot(
                w_ref[...].reshape(2 * STATES, 2 * STATES), columns, preferred_element_type=F32
            ).astype(BF16)
            for term in range(2):
                product = products[term * STATES : term * STATES + STATES]
                at = term * STATES + part * HALF
                lhs_ref[0:STATES, at : at + HALF] = product
                other = term * STATES + (1 - part) * HALF
                lhs_ref[STATES:, other : other + HALF] = product if part else -product
        lanes = [pl.ds(pl.multiple_of(part * STATES + tile * HALF, HALF), HALF) for part in range(2)]
        writes = []
        for out in range(2):
            columns = [w_ref[term, out * HALF : out * HALF + HALF, lanes[part]] for term in range(2) for part in range(2)]
            total = lax.dot_general(
                lhs_ref[...],
                jnp.concatenate(columns, axis=1),
                (((1,), (1,)), ((), ())),
                preferred_element_type=F32,
            )
            if partial is None:
                o_ref[out] = total
                continue
            out_ref[out] = (total + p_ref[out]).astype(BF16).reshape(2, STATES, HALF)
            first = (lax.axis_index("x0") ^ 1) * STATES + out * HALF
            goal = o_ref.at[:, :, pl.ds(pl.multiple_of(first, HALF), HALF)]
            writes.append(pltpu.make_async_copy(out_ref.at[out], goal, sem.at[out]))
            writes[-1].start()
        for write in writes:
            write.wait()

    scratch = [pltpu.VMEM((2, 2, HALF, HALF), BF16), pltpu.VMEM((2 * STATES, 2 * STATES), BF16)]
    if partial is None:
        args, specs, out_spec, aliases = (), [], IN_VMEM, {}
        out_shape = jax.ShapeDtypeStruct((2, 2 * STATES, HALF), F32)
    else:
        args, specs, out_spec, aliases = (partial, earlier), [IN_VMEM, IN_HBM], IN_HBM, {4: 0}
        out_shape = jax.ShapeDtypeStruct((2, STATES, 2 * STATES), BF16)
        scratch += [pltpu.VMEM((2, 2, STATES, HALF), BF16), pltpu.SemaphoreType.DMA((2,))]
    return pl.pallas_call(
        kernel,
        in_specs=[IN_VMEM] * 3 + specs,
        out_specs=out_spec,
        scratch_shapes=scratch,
        out_shape=out_shape,
        input_output_aliases=aliases,
        compiler_params=pltpu.CompilerParams(vmem_limit_bytes=VMEM),
        cost_estimate=LIGHT,
        name="section_2_half",
    )(*pieces, weights, *args)


def route(d1, d2, d3):
    pairs = []
    for device in range(128):
        ylo, z1, z0, core, x1, x0, yhi = (device >> place & 1 for place in range(6, -1, -1))
        goal = 0
        for bit in (yhi ^ ylo, z1 ^ d1, z0 ^ d3, ylo, x0, x1 ^ d2, core):
            goal = goal * 2 + bit
        pairs.append((device, goal))
    return pairs


def body(density, kraus, targets):
    packed = pack(density).reshape(32, 2, 64, 256)
    arrived = lax.all_to_all(packed, GATHERED, split_axis=0, concat_axis=0, tiled=True)
    arrived = arrived.reshape(8, 4, 2, 64, 256)
    weights = [operators(kraus, targets, section) for section in range(SECTIONS)]
    weights = list(lax.optimization_barrier(weights))
    kept, sent = first_section(arrived, weights[0])
    swapped = lax.ppermute(sent, "core", [(0, 1), (1, 0)])
    landed = {}
    for d3 in range(2):
        pieces = second_section(kept, swapped, weights[1], d3)
        for d2, d1 in itertools.product(range(2), repeat=2):
            landed[d1, d2, d3] = lax.ppermute(pieces[d1 * 2 + d2], AXES, route(d1, d2, d3))
    pieces = [landed[d1, 0, d3] for d1, d3 in itertools.product(range(2), repeat=2)]
    out = third_section(pieces, weights[2])
    partial = None
    for d3 in range(2):
        pieces = [landed[d1, 1, d3] for d1 in range(2)]
        partial = third_section_half(pieces, weights[2], d3, partial, out)
    return partial


def solution(mesh):
    fine = Mesh(mesh.devices.reshape((2,) * len(AXES)), AXES)
    split = P(None, AXES[:4], AXES[4:])
    return jax.shard_map(body, mesh=fine, in_specs=(split, P(), P()), out_specs=split, check_vma=False)
```

```python
import itertools

import jax
import jax.numpy as jnp
from jax import lax
from jax.experimental import pallas as pl
from jax.experimental.pallas import tpu as pltpu
from jax.sharding import Mesh
from jax.sharding import PartitionSpec as P

STATES = 512
QUBITS = 9
SECTIONS = 3
HALF = 256
BF16 = jnp.bfloat16
F32 = jnp.float32
AXES = ("ylo", "z1", "z0", "core", "x1", "x0", "yhi")
GATHERED = ("z1", "z0", "core", "x0", "yhi")
VMEM = 20 * 2**20
IN_VMEM = pl.BlockSpec(memory_space=pltpu.VMEM)
IN_HBM = pl.BlockSpec(memory_space=pltpu.HBM)


def cost(flops, data):
    return pl.CostEstimate(flops=flops, bytes_accessed=data, transcendentals=0)


LIGHT = cost(2**26, 2**16)


def pack(density):
    def kernel(x_ref, o_ref, in_ref, out_ref, sem):
        ylo = lax.axis_index("ylo")
        reads, writes = [], []
        for step in range(4):
            rows = pl.ds(step * 128, 128)
            reads.append(pltpu.make_async_copy(x_ref.at[:, rows], in_ref.at[step], sem.at[0, step]))
            reads[-1].start()
        for step in range(4):
            b8, b7 = step >> 1, step & 1
            reads[step].wait()
            for b6, low, high, top in itertools.product(range(2), repeat=4):
                lanes = (top * 4 + high * 2 + low) * 128
                tile = in_ref[step, :, b6 * 64 : b6 * 64 + 64, lanes : lanes + 128]
                out_ref[step, low, b6, high, :, :, top * 128 : top * 128 + 128] = tile
            writes.append(pltpu.make_async_copy(out_ref.at[step], o_ref.at[b7, :, :, :, b8 ^ ylo], sem.at[1, step]))
            writes[-1].start()
        for write in writes:
            write.wait()

    return pl.pallas_call(
        kernel,
        in_specs=[IN_HBM],
        out_specs=IN_HBM,
        out_shape=jax.ShapeDtypeStruct((2, 2, 2, 2, 2, 2, 64, 256), BF16),
        scratch_shapes=[
            pltpu.VMEM((4, 2, 128, 1024), BF16),
            pltpu.VMEM((4, 2, 2, 2, 2, 64, 256), BF16),
            pltpu.SemaphoreType.DMA((2, 4)),
        ],
        compiler_params=pltpu.CompilerParams(vmem_limit_bytes=62 * 2**20),
        cost_estimate=cost(0, 2**22),
        name="pack",
    )(density)


def operators(kraus, targets, section):
    def kernel(t_ref, k_ref, o_ref):
        def order(state):
            total = jnp.zeros_like(state)
            for bit in range(QUBITS):
                total += ((state >> t_ref[section, bit]) & 1) << bit
            return total

        out_state = lax.broadcasted_iota(jnp.int32, (STATES, 1), 0)
        in_state = lax.broadcasted_iota(jnp.int32, (1, STATES), 1)
        if section == 0:
            in_state = ((in_state >> 5 & 1) << 8) | ((in_state >> 6 & 7) << 5) | (in_state & 31)
        lanes = lax.broadcasted_iota(jnp.int32, (STATES, STATES), 1)
        rows = lax.broadcasted_iota(jnp.int32, (STATES, STATES), 0)
        left = (order(out_state) == lanes).astype(F32).astype(BF16)
        right = (order(in_state) == rows).astype(F32).astype(BF16)
        for part in range(2):
            picked = jnp.dot(left, k_ref[0, 0, part], preferred_element_type=F32).astype(BF16)
            at = part * STATES
            o_ref[0, :, at : at + STATES] = jnp.dot(picked, right, preferred_element_type=F32).astype(BF16)

    return pl.pallas_call(
        kernel,
        grid=(2,),
        in_specs=[
            pl.BlockSpec(memory_space=pltpu.SMEM),
            pl.BlockSpec((1, 1, 2, STATES, STATES), lambda term: (section, term, 0, 0, 0)),
        ],
        out_specs=pl.BlockSpec((1, STATES, 2 * STATES), lambda term: (term, 0, 0)),
        out_shape=jax.ShapeDtypeStruct((2, STATES, 2 * STATES), BF16),
        compiler_params=pltpu.CompilerParams(vmem_limit_bytes=54 * 2**20),
        cost_estimate=cost(8 * 2 * 512**3, 4 * 2**20),
        name="operators",
    )(targets, kraus)


def left(x, w_ref, lhs_ref, tiles=(0, 1)):
    for tile in tiles:
        for part in range(2):
            if part == 0:
                columns = jnp.concatenate([x(tile, 0), -x(tile, 1)], axis=0)
            else:
                columns = jnp.concatenate([x(tile, 1), x(tile, 0)], axis=0)
            products = jnp.dot(
                w_ref[...].reshape(2 * STATES, 2 * STATES), columns, preferred_element_type=F32
            ).astype(BF16)
            for term in range(2):
                product = products[term * STATES : term * STATES + STATES]
                at = term * 1024 + part * STATES + tile * HALF
                lhs_ref[0:STATES, at : at + HALF] = product
                other = term * 1024 + (1 - part) * STATES + tile * HALF
                lhs_ref[STATES:, other : other + HALF] = product if part else -product


def right(lhs, w_ref, emit):
    for tile in range(2):
        total = lax.dot_general(
            lhs[...],
            jnp.concatenate([w_ref[term, tile * HALF : tile * HALF + HALF] for term in range(2)], axis=1),
            (((1,), (1,)), ((), ())),
            preferred_element_type=F32,
        )
        emit(tile, total.astype(BF16))


def first_section(arrived, weights):
    def kernel(a_hbm, w_ref, keep_ref, send_ref, a_ref, x_ref, lhs_ref, out_ref, sem):
        core = lax.axis_index("core")
        reads = [pltpu.make_async_copy(a_hbm.at[:, col], a_ref.at[col], sem.at[col]) for col in range(4)]
        for read in reads:
            read.start()
        for tile in range(2):
            for col in (2 * tile, 2 * tile + 1):
                reads[col].wait()
                for source, part in itertools.product(range(8), range(2)):
                    low = a_ref[col, source, part, :, 0:128]
                    high = a_ref[col, source, part, :, 128:256]
                    rows = slice(source * 64, source * 64 + 64)
                    lanes = slice((col & 1) * 128, (col & 1) * 128 + 128)
                    x_ref[0, tile, part, rows, lanes] = jnp.concatenate([low[:, :64], high[:, :64]], axis=1)
                    x_ref[1, tile, part, rows, lanes] = jnp.concatenate([low[:, 64:], high[:, 64:]], axis=1)
            for step in range(2):
                left(lambda tile, part: x_ref[step, tile, part], w_ref, lhs_ref.at[step], (tile,))

        for step in range(2):

            def emit(tile, value):
                out_ref[step, tile] = value.reshape(2, 2, HALF, HALF)

            right(lhs_ref.at[step], w_ref, emit)
            for low, part in itertools.product(range(2), repeat=2):
                keep_ref[low, part, step] = out_ref[step, core, part, low]
                send_ref[low, part, step] = out_ref[step, 1 - core, part, low]

    half = jax.ShapeDtypeStruct((2, 2, 2, HALF, HALF), BF16)
    return pl.pallas_call(
        kernel,
        in_specs=[IN_HBM, IN_VMEM],
        out_specs=[IN_VMEM] * 2,
        scratch_shapes=[
            pltpu.VMEM((4, 8, 2, 64, 256), BF16),
            pltpu.VMEM((2, 2, 2, STATES, HALF), BF16),
            pltpu.VMEM((2, 2 * STATES, 4 * STATES), BF16),
            pltpu.VMEM((2, 2, 2, 2, HALF, HALF), BF16),
            pltpu.SemaphoreType.DMA((4,)),
        ],
        out_shape=[half, half],
        compiler_params=pltpu.CompilerParams(vmem_limit_bytes=32 * 2**20),
        cost_estimate=LIGHT,
        name="section_0",
    )(arrived, weights)


def second_section(kept, arrived, weights, turn):
    def kernel(k_ref, a_ref, w_ref, o00, o01, o10, o11, x_ref, lhs_ref, out_ref):
        core, z1, x1 = lax.axis_index("core"), lax.axis_index("z1"), lax.axis_index("x1")
        low = lax.axis_index("z0") ^ turn
        for tile, part in itertools.product(range(2), repeat=2):
            x_ref[tile, part, core] = k_ref[low, part, tile]
            x_ref[tile, part, 1 - core] = a_ref[low, part, tile]

        def emit(tile, value):
            out_ref[tile] = value.reshape(2, 2, HALF, HALF)

        left(lambda tile, part: x_ref[tile, part].reshape(STATES, HALF), w_ref, lhs_ref)
        right(lhs_ref, w_ref, emit)
        for d, o_ref in enumerate((o00, o01, o10, o11)):
            o_ref[...] = out_ref[x1 ^ (d & 1), :, z1 ^ (d >> 1)]

    piece = jax.ShapeDtypeStruct((2, HALF, HALF), BF16)
    return pl.pallas_call(
        kernel,
        in_specs=[IN_VMEM] * 3,
        out_specs=[IN_VMEM] * 4,
        scratch_shapes=[
            pltpu.VMEM((2, 2, 2, HALF, HALF), BF16),
            pltpu.VMEM((2 * STATES, 4 * STATES), BF16),
            pltpu.VMEM((2, 2, 2, HALF, HALF), BF16),
        ],
        out_shape=[piece] * 4,
        compiler_params=pltpu.CompilerParams(vmem_limit_bytes=VMEM),
        cost_estimate=LIGHT,
        name="section_1",
    )(kept, arrived, weights)


def third_section(pieces, weights, turn, partials=None):
    def kernel(a00, a01, a10, a11, w_ref, *rest):
        if partials is None:
            o_ref, x_ref, lhs_ref = rest
        else:
            p_ref, o_ref, x_ref, lhs_ref, out_ref, sem = rest
        z1, tile = lax.axis_index("z1"), lax.axis_index("z0") ^ turn
        lanes = [pl.ds(pl.multiple_of(part * STATES + tile * HALF, HALF), HALF) for part in range(2)]
        writes = []
        for side, (a0, a1) in enumerate(((a00, a10), (a01, a11))):
            for d, a_ref in enumerate((a0, a1)):
                for part in range(2):
                    x_ref[side, part, z1 ^ d] = a_ref[part]
            real, imag = (x_ref[side, part].reshape(STATES, HALF) for part in range(2))
            for part in range(2):
                columns = jnp.concatenate([imag, real] if part else [real, -imag], axis=0)
                products = jnp.dot(
                    w_ref[...].reshape(2 * STATES, 2 * STATES), columns, preferred_element_type=F32
                ).astype(BF16)
                for term in range(2):
                    product = products[term * STATES : term * STATES + STATES]
                    at = term * STATES + part * HALF
                    lhs_ref[side, 0:STATES, at : at + HALF] = product
                    other = term * STATES + (1 - part) * HALF
                    lhs_ref[side, STATES:, other : other + HALF] = product if part else -product
            for out in range(2):
                columns = [
                    w_ref[term, out * HALF : out * HALF + HALF, lanes[part]] for term in range(2) for part in range(2)
                ]
                total = lax.dot_general(
                    lhs_ref[side],
                    jnp.concatenate(columns, axis=1),
                    (((1,), (1,)), ((), ())),
                    preferred_element_type=F32,
                )
                if partials is None:
                    o_ref[side, out] = total
                    continue
                out_ref[side, out] = (total + p_ref[side, out]).astype(BF16).reshape(2, STATES, HALF)
                first = (lax.axis_index("x0") ^ side) * STATES + out * HALF
                goal = o_ref.at[:, :, pl.ds(pl.multiple_of(first, HALF), HALF)]
                writes.append(pltpu.make_async_copy(out_ref.at[side, out], goal, sem.at[side, out]))
                writes[-1].start()
        for write in writes:
            write.wait()

    scratch = [pltpu.VMEM((2, 2, 2, HALF, HALF), BF16), pltpu.VMEM((2, 2 * STATES, 2 * STATES), BF16)]
    args = (*pieces, weights)
    if partials is None:
        out_spec, out_shape = IN_VMEM, jax.ShapeDtypeStruct((2, 2, 2 * STATES, HALF), F32)
    else:
        args += (partials,)
        out_spec, out_shape = IN_HBM, jax.ShapeDtypeStruct((2, STATES, 2 * STATES), BF16)
        scratch += [pltpu.VMEM((2, 2, 2, STATES, HALF), BF16), pltpu.SemaphoreType.DMA((2, 2))]
    return pl.pallas_call(
        kernel,
        in_specs=[IN_VMEM] * len(args),
        out_specs=out_spec,
        scratch_shapes=scratch,
        out_shape=out_shape,
        compiler_params=pltpu.CompilerParams(vmem_limit_bytes=VMEM),
        cost_estimate=LIGHT,
        name="section_2",
    )(*args)


def route(d1, d2, d3):
    pairs = []
    for device in range(128):
        ylo, z1, z0, core, x1, x0, yhi = (device >> place & 1 for place in range(6, -1, -1))
        goal = 0
        for bit in (yhi ^ ylo, z1 ^ d1, z0 ^ d3, ylo, x0, x1 ^ d2, core):
            goal = goal * 2 + bit
        pairs.append((device, goal))
    return pairs


def body(density, kraus, targets):
    packed = pack(density).reshape(32, 2, 64, 256)
    arrived = lax.all_to_all(packed, GATHERED, split_axis=0, concat_axis=0, tiled=True)
    arrived = arrived.reshape(8, 4, 2, 64, 256)
    weights = [operators(kraus, targets, section) for section in range(SECTIONS)]
    weights = list(lax.optimization_barrier(weights))
    kept, sent = first_section(arrived, weights[0])
    swapped = lax.ppermute(sent, "core", [(0, 1), (1, 0)])
    landed = {}
    for d3 in range(2):
        pieces = second_section(kept, swapped, weights[1], d3)
        for d2, d1 in itertools.product(range(2), repeat=2):
            landed[d1, d2, d3] = lax.ppermute(pieces[d1 * 2 + d2], AXES, route(d1, d2, d3))
    out = None
    for d3 in range(2):
        pieces = [landed[d1, d2, d3] for d1, d2 in itertools.product(range(2), repeat=2)]
        out = third_section(pieces, weights[2], d3, out)
    return out


def solution(mesh):
    fine = Mesh(mesh.devices.reshape((2,) * len(AXES)), AXES)
    split = P(None, AXES[:4], AXES[4:])
    return jax.shard_map(body, mesh=fine, in_specs=(split, P(), P()), out_specs=split, check_vma=False)
```

```python
import itertools

import jax
import jax.numpy as jnp
from jax import lax
from jax.experimental import pallas as pl
from jax.experimental.pallas import tpu as pltpu
from jax.sharding import Mesh
from jax.sharding import PartitionSpec as P

STATES = 512
QUBITS = 9
SECTIONS = 3
HALF = 256
BF16 = jnp.bfloat16
F32 = jnp.float32
AXES = ("ylo", "z1", "z0", "core", "x1", "x0", "yhi")
GATHERED = ("z1", "z0", "core", "x0", "yhi")
VMEM = 20 * 2**20
IN_VMEM = pl.BlockSpec(memory_space=pltpu.VMEM)
IN_HBM = pl.BlockSpec(memory_space=pltpu.HBM)


def cost(flops, data):
    return pl.CostEstimate(flops=flops, bytes_accessed=data, transcendentals=0)


LIGHT = cost(2**26, 2**16)


def pack(density):
    def kernel(x_ref, o_ref, in_ref, out_ref, sem):
        ylo = lax.axis_index("ylo")
        reads, writes = [], []
        for step in range(4):
            rows = pl.ds(step * 128, 128)
            reads.append(pltpu.make_async_copy(x_ref.at[:, rows], in_ref.at[step], sem.at[0, step]))
            reads[-1].start()
        for step in range(4):
            b8, b7 = step >> 1, step & 1
            reads[step].wait()
            for b6, low, high, top in itertools.product(range(2), repeat=4):
                lanes = (top * 4 + high * 2 + low) * 128
                tile = in_ref[step, :, b6 * 64 : b6 * 64 + 64, lanes : lanes + 128]
                out_ref[step, low, b6, high, :, :, top * 128 : top * 128 + 128] = tile
            writes.append(pltpu.make_async_copy(out_ref.at[step], o_ref.at[b7, :, :, :, b8 ^ ylo], sem.at[1, step]))
            writes[-1].start()
        for write in writes:
            write.wait()

    return pl.pallas_call(
        kernel,
        in_specs=[IN_HBM],
        out_specs=IN_HBM,
        out_shape=jax.ShapeDtypeStruct((2, 2, 2, 2, 2, 2, 64, 256), BF16),
        scratch_shapes=[
            pltpu.VMEM((4, 2, 128, 1024), BF16),
            pltpu.VMEM((4, 2, 2, 2, 2, 64, 256), BF16),
            pltpu.SemaphoreType.DMA((2, 4)),
        ],
        compiler_params=pltpu.CompilerParams(vmem_limit_bytes=62 * 2**20),
        cost_estimate=cost(0, 2**22),
        name="pack",
    )(density)


def operators(kraus, targets, section):
    def kernel(t_ref, k_ref, o_ref):
        def order(state):
            total = jnp.zeros_like(state)
            for bit in range(QUBITS):
                total += ((state >> t_ref[section, bit]) & 1) << bit
            return total

        out_state = lax.broadcasted_iota(jnp.int32, (STATES, 1), 0)
        in_state = lax.broadcasted_iota(jnp.int32, (1, STATES), 1)
        if section == 0:
            in_state = ((in_state >> 5 & 1) << 8) | ((in_state >> 6 & 7) << 5) | (in_state & 31)
        lanes = lax.broadcasted_iota(jnp.int32, (STATES, STATES), 1)
        rows = lax.broadcasted_iota(jnp.int32, (STATES, STATES), 0)
        left = (order(out_state) == lanes).astype(F32).astype(BF16)
        right = (order(in_state) == rows).astype(F32).astype(BF16)
        for part in range(2):
            picked = jnp.dot(left, k_ref[0, 0, part], preferred_element_type=F32).astype(BF16)
            at = part * STATES
            o_ref[0, :, at : at + STATES] = jnp.dot(picked, right, preferred_element_type=F32).astype(BF16)

    return pl.pallas_call(
        kernel,
        grid=(2,),
        in_specs=[
            pl.BlockSpec(memory_space=pltpu.SMEM),
            pl.BlockSpec((1, 1, 2, STATES, STATES), lambda term: (section, term, 0, 0, 0)),
        ],
        out_specs=pl.BlockSpec((1, STATES, 2 * STATES), lambda term: (term, 0, 0)),
        out_shape=jax.ShapeDtypeStruct((2, STATES, 2 * STATES), BF16),
        compiler_params=pltpu.CompilerParams(vmem_limit_bytes=54 * 2**20),
        cost_estimate=cost(8 * 2 * 512**3, 4 * 2**20),
        name="operators",
    )(targets, kraus)


def left(x, w_ref, lhs_ref, tiles=(0, 1)):
    for tile in tiles:
        for part in range(2):
            if part == 0:
                columns = jnp.concatenate([x(tile, 0), -x(tile, 1)], axis=0)
            else:
                columns = jnp.concatenate([x(tile, 1), x(tile, 0)], axis=0)
            products = jnp.dot(
                w_ref[...].reshape(2 * STATES, 2 * STATES), columns, preferred_element_type=F32
            ).astype(BF16)
            for term in range(2):
                product = products[term * STATES : term * STATES + STATES]
                at = term * 1024 + part * STATES + tile * HALF
                lhs_ref[0:STATES, at : at + HALF] = product
                other = term * 1024 + (1 - part) * STATES + tile * HALF
                lhs_ref[STATES:, other : other + HALF] = product if part else -product


def right(lhs, w_ref, emit):
    for tile in range(2):
        total = lax.dot_general(
            lhs[...],
            jnp.concatenate([w_ref[term, tile * HALF : tile * HALF + HALF] for term in range(2)], axis=1),
            (((1,), (1,)), ((), ())),
            preferred_element_type=F32,
        )
        emit(tile, total.astype(BF16))


def first_section(arrived, weights):
    def kernel(a_hbm, w_ref, keep_ref, send_ref, a_ref, x_ref, lhs_ref, out_ref, sem):
        core = lax.axis_index("core")
        reads = [pltpu.make_async_copy(a_hbm.at[:, col], a_ref.at[col], sem.at[col]) for col in range(4)]
        for read in reads:
            read.start()
        for tile in range(2):
            for col in (2 * tile, 2 * tile + 1):
                reads[col].wait()
                for source, part in itertools.product(range(8), range(2)):
                    low = a_ref[col, source, part, :, 0:128]
                    high = a_ref[col, source, part, :, 128:256]
                    rows = slice(source * 64, source * 64 + 64)
                    lanes = slice((col & 1) * 128, (col & 1) * 128 + 128)
                    x_ref[0, tile, part, rows, lanes] = jnp.concatenate([low[:, :64], high[:, :64]], axis=1)
                    x_ref[1, tile, part, rows, lanes] = jnp.concatenate([low[:, 64:], high[:, 64:]], axis=1)
            for step in range(2):
                left(lambda tile, part: x_ref[step, tile, part], w_ref, lhs_ref.at[step], (tile,))

        for step in range(2):

            def emit(tile, value):
                out_ref[step, tile] = value.reshape(2, 2, HALF, HALF)

            right(lhs_ref.at[step], w_ref, emit)
            for low, part in itertools.product(range(2), repeat=2):
                keep_ref[low, part, step] = out_ref[step, core, part, low]
                send_ref[low, part, step] = out_ref[step, 1 - core, part, low]

    half = jax.ShapeDtypeStruct((2, 2, 2, HALF, HALF), BF16)
    return pl.pallas_call(
        kernel,
        in_specs=[IN_HBM, IN_VMEM],
        out_specs=[IN_VMEM] * 2,
        scratch_shapes=[
            pltpu.VMEM((4, 8, 2, 64, 256), BF16),
            pltpu.VMEM((2, 2, 2, STATES, HALF), BF16),
            pltpu.VMEM((2, 2 * STATES, 4 * STATES), BF16),
            pltpu.VMEM((2, 2, 2, 2, HALF, HALF), BF16),
            pltpu.SemaphoreType.DMA((4,)),
        ],
        out_shape=[half, half],
        compiler_params=pltpu.CompilerParams(vmem_limit_bytes=32 * 2**20),
        cost_estimate=LIGHT,
        name="section_0",
    )(arrived, weights)


def second_section(kept, arrived, weights, turn):
    def kernel(k_ref, a_ref, w_ref, o00, o01, o10, o11, x_ref, lhs_ref, out_ref):
        core, z1, x1 = lax.axis_index("core"), lax.axis_index("z1"), lax.axis_index("x1")
        low = lax.axis_index("z0") ^ turn
        for tile, part in itertools.product(range(2), repeat=2):
            x_ref[tile, part, core] = k_ref[low, part, tile]
            x_ref[tile, part, 1 - core] = a_ref[low, part, tile]

        def emit(tile, value):
            out_ref[tile] = value.reshape(2, 2, HALF, HALF)

        left(lambda tile, part: x_ref[tile, part].reshape(STATES, HALF), w_ref, lhs_ref)
        right(lhs_ref, w_ref, emit)
        for d, o_ref in enumerate((o00, o01, o10, o11)):
            o_ref[...] = out_ref[x1 ^ (d & 1), :, z1 ^ (d >> 1)]

    piece = jax.ShapeDtypeStruct((2, HALF, HALF), BF16)
    return pl.pallas_call(
        kernel,
        in_specs=[IN_VMEM] * 3,
        out_specs=[IN_VMEM] * 4,
        scratch_shapes=[
            pltpu.VMEM((2, 2, 2, HALF, HALF), BF16),
            pltpu.VMEM((2 * STATES, 4 * STATES), BF16),
            pltpu.VMEM((2, 2, 2, HALF, HALF), BF16),
        ],
        out_shape=[piece] * 4,
        compiler_params=pltpu.CompilerParams(vmem_limit_bytes=VMEM),
        cost_estimate=LIGHT,
        name="section_1",
    )(kept, arrived, weights)


def third_section(pieces, weights, turn, partials=None):
    def kernel(a00, a01, a10, a11, w_ref, *rest):
        if partials is None:
            o_ref, x_ref, lhs_ref = rest
        else:
            p_ref, o_ref, x_ref, lhs_ref, out_ref, sem = rest
        z1, tile = lax.axis_index("z1"), lax.axis_index("z0") ^ turn
        lanes = [pl.ds(pl.multiple_of(part * STATES + tile * HALF, HALF), HALF) for part in range(2)]
        writes = []
        for side, (a0, a1) in enumerate(((a00, a10), (a01, a11))):
            for d, a_ref in enumerate((a0, a1)):
                for part in range(2):
                    x_ref[side, part, z1 ^ d] = a_ref[part]
            real, imag = (x_ref[side, part].reshape(STATES, HALF) for part in range(2))
            for part in range(2):
                columns = jnp.concatenate([imag, real] if part else [real, -imag], axis=0)
                products = jnp.dot(
                    w_ref[...].reshape(2 * STATES, 2 * STATES), columns, preferred_element_type=F32
                ).astype(BF16)
                for term in range(2):
                    product = products[term * STATES : term * STATES + STATES]
                    at = term * STATES + part * HALF
                    lhs_ref[side, 0:STATES, at : at + HALF] = product
                    other = term * STATES + (1 - part) * HALF
                    lhs_ref[side, STATES:, other : other + HALF] = product if part else -product
            for out in range(2):
                columns = [
                    w_ref[term, out * HALF : out * HALF + HALF, lanes[part]] for term in range(2) for part in range(2)
                ]
                picked = jnp.concatenate(columns, axis=1)
                last = partials is not None and side == 1 and out == 1
                for part in range(2) if last else (slice(0, 2),):
                    rows = slice(part * STATES, part * STATES + STATES) if last else slice(0, 2 * STATES)
                    total = lax.dot_general(
                        lhs_ref[side, rows], picked, (((1,), (1,)), ((), ())), preferred_element_type=F32
                    )
                    if partials is None:
                        o_ref[side, out] = total
                        continue
                    parts = slice(part, part + 1) if last else part
                    total = (total + p_ref[side, out, rows]).astype(BF16)
                    out_ref[side, out, parts] = total.reshape(-1, STATES, HALF)
                    first = (lax.axis_index("x0") ^ side) * STATES + out * HALF
                    goal = o_ref.at[parts, :, pl.ds(pl.multiple_of(first, HALF), HALF)]
                    mark = sem.at[len(writes)]
                    writes.append(pltpu.make_async_copy(out_ref.at[side, out, parts], goal, mark))
                    writes[-1].start()
        for write in writes:
            write.wait()

    scratch = [pltpu.VMEM((2, 2, 2, HALF, HALF), BF16), pltpu.VMEM((2, 2 * STATES, 2 * STATES), BF16)]
    args = (*pieces, weights)
    if partials is None:
        out_spec, out_shape = IN_VMEM, jax.ShapeDtypeStruct((2, 2, 2 * STATES, HALF), F32)
    else:
        args += (partials,)
        out_spec, out_shape = IN_HBM, jax.ShapeDtypeStruct((2, STATES, 2 * STATES), BF16)
        scratch += [pltpu.VMEM((2, 2, 2, STATES, HALF), BF16), pltpu.SemaphoreType.DMA((5,))]
    return pl.pallas_call(
        kernel,
        in_specs=[IN_VMEM] * len(args),
        out_specs=out_spec,
        scratch_shapes=scratch,
        out_shape=out_shape,
        compiler_params=pltpu.CompilerParams(vmem_limit_bytes=VMEM),
        cost_estimate=LIGHT,
        name="section_2",
    )(*args)


def route(d1, d2, d3):
    pairs = []
    for device in range(128):
        ylo, z1, z0, core, x1, x0, yhi = (device >> place & 1 for place in range(6, -1, -1))
        goal = 0
        for bit in (yhi ^ ylo, z1 ^ d1, z0 ^ d3, ylo, x0, x1 ^ d2, core):
            goal = goal * 2 + bit
        pairs.append((device, goal))
    return pairs


def body(density, kraus, targets):
    packed = pack(density).reshape(32, 2, 64, 256)
    arrived = lax.all_to_all(packed, GATHERED, split_axis=0, concat_axis=0, tiled=True)
    arrived = arrived.reshape(8, 4, 2, 64, 256)
    weights = [operators(kraus, targets, section) for section in range(SECTIONS)]
    weights = list(lax.optimization_barrier(weights))
    kept, sent = first_section(arrived, weights[0])
    swapped = lax.ppermute(sent, "core", [(0, 1), (1, 0)])
    landed = {}
    for d3 in range(2):
        pieces = second_section(kept, swapped, weights[1], d3)
        for d2, d1 in itertools.product(range(2), repeat=2):
            landed[d1, d2, d3] = lax.ppermute(pieces[d1 * 2 + d2], AXES, route(d1, d2, d3))
    out = None
    for d3 in range(2):
        pieces = [landed[d1, d2, d3] for d1, d2 in itertools.product(range(2), repeat=2)]
        out = third_section(pieces, weights[2], d3, out)
    return out


def solution(mesh):
    fine = Mesh(mesh.devices.reshape((2,) * len(AXES)), AXES)
    split = P(None, AXES[:4], AXES[4:])
    return jax.shard_map(body, mesh=fine, in_specs=(split, P(), P()), out_specs=split, check_vma=False)
```

```python
import itertools

import jax
import jax.numpy as jnp
from jax import lax
from jax.experimental import pallas as pl
from jax.experimental.pallas import tpu as pltpu
from jax.sharding import Mesh
from jax.sharding import PartitionSpec as P

STATES = 512
QUBITS = 9
SECTIONS = 3
HALF = 256
BF16 = jnp.bfloat16
F32 = jnp.float32
AXES = ("ylo", "z1", "z0", "core", "x1", "x0", "yhi")
GATHERED = ("z1", "z0", "core", "x0", "yhi")
VMEM = 20 * 2**20
IN_VMEM = pl.BlockSpec(memory_space=pltpu.VMEM)
IN_HBM = pl.BlockSpec(memory_space=pltpu.HBM)


def cost(flops, data):
    return pl.CostEstimate(flops=flops, bytes_accessed=data, transcendentals=0)


LIGHT = cost(2**26, 2**16)


def pack(density):
    def kernel(x_ref, o_ref, in_ref, out_ref, sem):
        ylo = lax.axis_index("ylo")
        reads, writes = [], []
        for step in range(4):
            rows = pl.ds(step * 128, 128)
            reads.append(pltpu.make_async_copy(x_ref.at[:, rows], in_ref.at[step], sem.at[0, step]))
            reads[-1].start()
        for step in range(4):
            b8, b7 = step >> 1, step & 1
            reads[step].wait()
            for b6, low, high, top in itertools.product(range(2), repeat=4):
                lanes = (top * 4 + high * 2 + low) * 128
                tile = in_ref[step, :, b6 * 64 : b6 * 64 + 64, lanes : lanes + 128]
                out_ref[step, low, b6, high, :, :, top * 128 : top * 128 + 128] = tile
            writes.append(pltpu.make_async_copy(out_ref.at[step], o_ref.at[b7, :, :, :, b8 ^ ylo], sem.at[1, step]))
            writes[-1].start()
        for write in writes:
            write.wait()

    return pl.pallas_call(
        kernel,
        in_specs=[IN_HBM],
        out_specs=IN_HBM,
        out_shape=jax.ShapeDtypeStruct((2, 2, 2, 2, 2, 2, 64, 256), BF16),
        scratch_shapes=[
            pltpu.VMEM((4, 2, 128, 1024), BF16),
            pltpu.VMEM((4, 2, 2, 2, 2, 64, 256), BF16),
            pltpu.SemaphoreType.DMA((2, 4)),
        ],
        compiler_params=pltpu.CompilerParams(vmem_limit_bytes=62 * 2**20),
        cost_estimate=cost(0, 2**22),
        name="pack",
    )(density)


def operators(kraus, targets, section):
    def kernel(t_ref, k_ref, o_ref):
        def order(state):
            total = jnp.zeros_like(state)
            for bit in range(QUBITS):
                total += ((state >> t_ref[section, bit]) & 1) << bit
            return total

        out_state = lax.broadcasted_iota(jnp.int32, (STATES, 1), 0)
        in_state = lax.broadcasted_iota(jnp.int32, (1, STATES), 1)
        if section == 0:
            in_state = ((in_state >> 5 & 1) << 8) | ((in_state >> 6 & 7) << 5) | (in_state & 31)
        lanes = lax.broadcasted_iota(jnp.int32, (STATES, STATES), 1)
        rows = lax.broadcasted_iota(jnp.int32, (STATES, STATES), 0)
        left = (order(out_state) == lanes).astype(F32).astype(BF16)
        right = (order(in_state) == rows).astype(F32).astype(BF16)
        for part in range(2):
            picked = jnp.dot(left, k_ref[0, 0, part], preferred_element_type=F32).astype(BF16)
            at = part * STATES
            o_ref[0, :, at : at + STATES] = jnp.dot(picked, right, preferred_element_type=F32).astype(BF16)

    return pl.pallas_call(
        kernel,
        grid=(2,),
        in_specs=[
            pl.BlockSpec(memory_space=pltpu.SMEM),
            pl.BlockSpec((1, 1, 2, STATES, STATES), lambda term: (section, term, 0, 0, 0)),
        ],
        out_specs=pl.BlockSpec((1, STATES, 2 * STATES), lambda term: (term, 0, 0)),
        out_shape=jax.ShapeDtypeStruct((2, STATES, 2 * STATES), BF16),
        compiler_params=pltpu.CompilerParams(vmem_limit_bytes=54 * 2**20),
        cost_estimate=cost(8 * 2 * 512**3, 4 * 2**20),
        name="operators",
    )(targets, kraus)


def left(x, w_ref, lhs_ref, tiles=(0, 1)):
    for tile in tiles:
        for part in range(2):
            if part == 0:
                columns = jnp.concatenate([x(tile, 0), -x(tile, 1)], axis=0)
            else:
                columns = jnp.concatenate([x(tile, 1), x(tile, 0)], axis=0)
            products = jnp.dot(
                w_ref[...].reshape(2 * STATES, 2 * STATES), columns, preferred_element_type=F32
            ).astype(BF16)
            for term in range(2):
                product = products[term * STATES : term * STATES + STATES]
                at = term * 1024 + part * STATES + tile * HALF
                lhs_ref[0:STATES, at : at + HALF] = product
                other = term * 1024 + (1 - part) * STATES + tile * HALF
                lhs_ref[STATES:, other : other + HALF] = product if part else -product


def right(lhs, w_ref, emit):
    for tile in range(2):
        total = lax.dot_general(
            lhs[...],
            jnp.concatenate([w_ref[term, tile * HALF : tile * HALF + HALF] for term in range(2)], axis=1),
            (((1,), (1,)), ((), ())),
            preferred_element_type=F32,
        )
        emit(tile, total.astype(BF16))


def first_section(arrived, weights):
    def kernel(a_hbm, w_ref, keep_ref, send_ref, a_ref, x_ref, lhs_ref, out_ref, sem):
        core = lax.axis_index("core")
        reads = [
            pltpu.make_async_copy(a_hbm.at[rows, col], a_ref.at[col, rows], sem.at[col, at])
            for col in range(4)
            for at, rows in enumerate((pl.ds(0, 4), pl.ds(4, 4)))
        ]
        for read in reads:
            read.start()
        for tile in range(2):
            for col in (2 * tile, 2 * tile + 1):
                for source, part in itertools.product(range(8), range(2)):
                    if source % 4 == 0 and part == 0:
                        reads[col * 2 + source // 4].wait()
                    low = a_ref[col, source, part, :, 0:128]
                    high = a_ref[col, source, part, :, 128:256]
                    rows = slice(source * 64, source * 64 + 64)
                    lanes = slice((col & 1) * 128, (col & 1) * 128 + 128)
                    x_ref[0, tile, part, rows, lanes] = jnp.concatenate([low[:, :64], high[:, :64]], axis=1)
                    x_ref[1, tile, part, rows, lanes] = jnp.concatenate([low[:, 64:], high[:, 64:]], axis=1)
            for step in range(2):
                left(lambda tile, part: x_ref[step, tile, part], w_ref, lhs_ref.at[step], (tile,))

        for step in range(2):

            def emit(tile, value):
                out_ref[step, tile] = value.reshape(2, 2, HALF, HALF)

            right(lhs_ref.at[step], w_ref, emit)
            for low, part in itertools.product(range(2), repeat=2):
                keep_ref[low, part, step] = out_ref[step, core, part, low]
                send_ref[low, part, step] = out_ref[step, 1 - core, part, low]

    half = jax.ShapeDtypeStruct((2, 2, 2, HALF, HALF), BF16)
    return pl.pallas_call(
        kernel,
        in_specs=[IN_HBM, IN_VMEM],
        out_specs=[IN_VMEM] * 2,
        scratch_shapes=[
            pltpu.VMEM((4, 8, 2, 64, 256), BF16),
            pltpu.VMEM((2, 2, 2, STATES, HALF), BF16),
            pltpu.VMEM((2, 2 * STATES, 4 * STATES), BF16),
            pltpu.VMEM((2, 2, 2, 2, HALF, HALF), BF16),
            pltpu.SemaphoreType.DMA((4, 2)),
        ],
        out_shape=[half, half],
        compiler_params=pltpu.CompilerParams(vmem_limit_bytes=32 * 2**20),
        cost_estimate=LIGHT,
        name="section_0",
    )(arrived, weights)


def second_section(kept, arrived, weights, turn):
    def kernel(k_ref, a_ref, w_ref, o00, o01, o10, o11, x_ref, lhs_ref, out_ref):
        core, z1, x1 = lax.axis_index("core"), lax.axis_index("z1"), lax.axis_index("x1")
        low = lax.axis_index("z0") ^ turn
        for tile, part in itertools.product(range(2), repeat=2):
            x_ref[tile, part, core] = k_ref[low, part, tile]
            x_ref[tile, part, 1 - core] = a_ref[low, part, tile]

        def emit(tile, value):
            out_ref[tile] = value.reshape(2, 2, HALF, HALF)

        left(lambda tile, part: x_ref[tile, part].reshape(STATES, HALF), w_ref, lhs_ref)
        right(lhs_ref, w_ref, emit)
        for d, o_ref in enumerate((o00, o01, o10, o11)):
            o_ref[...] = out_ref[x1 ^ (d & 1), :, z1 ^ (d >> 1)]

    piece = jax.ShapeDtypeStruct((2, HALF, HALF), BF16)
    return pl.pallas_call(
        kernel,
        in_specs=[IN_VMEM] * 3,
        out_specs=[IN_VMEM] * 4,
        scratch_shapes=[
            pltpu.VMEM((2, 2, 2, HALF, HALF), BF16),
            pltpu.VMEM((2 * STATES, 4 * STATES), BF16),
            pltpu.VMEM((2, 2, 2, HALF, HALF), BF16),
        ],
        out_shape=[piece] * 4,
        compiler_params=pltpu.CompilerParams(vmem_limit_bytes=VMEM),
        cost_estimate=LIGHT,
        name="section_1",
    )(kept, arrived, weights)


def third_section(pieces, weights, turn, partials=None):
    def kernel(a00, a01, a10, a11, w_ref, *rest):
        if partials is None:
            o_ref, x_ref, lhs_ref = rest
        else:
            p_ref, o_ref, x_ref, lhs_ref, out_ref, sem = rest
        z1, tile = lax.axis_index("z1"), lax.axis_index("z0") ^ turn
        lanes = [pl.ds(pl.multiple_of(part * STATES + tile * HALF, HALF), HALF) for part in range(2)]
        writes = []
        for side, (a0, a1) in enumerate(((a00, a10), (a01, a11))):
            for d, a_ref in enumerate((a0, a1)):
                for part in range(2):
                    x_ref[side, part, z1 ^ d] = a_ref[part]
            real, imag = (x_ref[side, part].reshape(STATES, HALF) for part in range(2))
            for part in range(2):
                columns = jnp.concatenate([imag, real] if part else [real, -imag], axis=0)
                products = jnp.dot(
                    w_ref[...].reshape(2 * STATES, 2 * STATES), columns, preferred_element_type=F32
                ).astype(BF16)
                for term in range(2):
                    product = products[term * STATES : term * STATES + STATES]
                    at = term * STATES + part * HALF
                    lhs_ref[side, 0:STATES, at : at + HALF] = product
                    other = term * STATES + (1 - part) * HALF
                    lhs_ref[side, STATES:, other : other + HALF] = product if part else -product
            for out in range(2):
                columns = [
                    w_ref[term, out * HALF : out * HALF + HALF, lanes[part]] for term in range(2) for part in range(2)
                ]
                picked = jnp.concatenate(columns, axis=1)
                last = partials is not None and side == 1 and out == 1
                for part in range(2) if last else (slice(0, 2),):
                    rows = slice(part * STATES, part * STATES + STATES) if last else slice(0, 2 * STATES)
                    total = lax.dot_general(
                        lhs_ref[side, rows], picked, (((1,), (1,)), ((), ())), preferred_element_type=F32
                    )
                    if partials is None:
                        o_ref[side, out] = total
                        continue
                    parts = slice(part, part + 1) if last else part
                    total = (total + p_ref[side, out, rows]).astype(BF16)
                    out_ref[side, out, parts] = total.reshape(-1, STATES, HALF)
                    first = (lax.axis_index("x0") ^ side) * STATES + out * HALF
                    goal = o_ref.at[parts, :, pl.ds(pl.multiple_of(first, HALF), HALF)]
                    mark = sem.at[len(writes)]
                    writes.append(pltpu.make_async_copy(out_ref.at[side, out, parts], goal, mark))
                    writes[-1].start()
        for write in writes:
            write.wait()

    scratch = [pltpu.VMEM((2, 2, 2, HALF, HALF), BF16), pltpu.VMEM((2, 2 * STATES, 2 * STATES), BF16)]
    args = (*pieces, weights)
    if partials is None:
        out_spec, out_shape = IN_VMEM, jax.ShapeDtypeStruct((2, 2, 2 * STATES, HALF), F32)
    else:
        args += (partials,)
        out_spec, out_shape = IN_HBM, jax.ShapeDtypeStruct((2, STATES, 2 * STATES), BF16)
        scratch += [pltpu.VMEM((2, 2, 2, STATES, HALF), BF16), pltpu.SemaphoreType.DMA((5,))]
    return pl.pallas_call(
        kernel,
        in_specs=[IN_VMEM] * len(args),
        out_specs=out_spec,
        scratch_shapes=scratch,
        out_shape=out_shape,
        compiler_params=pltpu.CompilerParams(vmem_limit_bytes=VMEM),
        cost_estimate=LIGHT,
        name="section_2",
    )(*args)


def route(d1, d2, d3):
    pairs = []
    for device in range(128):
        ylo, z1, z0, core, x1, x0, yhi = (device >> place & 1 for place in range(6, -1, -1))
        goal = 0
        for bit in (yhi ^ ylo, z1 ^ d1, z0 ^ d3, ylo, x0, x1 ^ d2, core):
            goal = goal * 2 + bit
        pairs.append((device, goal))
    return pairs


def body(density, kraus, targets):
    packed = pack(density).reshape(32, 2, 64, 256)
    arrived = lax.all_to_all(packed, GATHERED, split_axis=0, concat_axis=0, tiled=True)
    arrived = arrived.reshape(8, 4, 2, 64, 256)
    weights = [operators(kraus, targets, section) for section in range(SECTIONS)]
    weights = list(lax.optimization_barrier(weights))
    kept, sent = first_section(arrived, weights[0])
    swapped = lax.ppermute(sent, "core", [(0, 1), (1, 0)])
    landed = {}
    for d3 in range(2):
        pieces = second_section(kept, swapped, weights[1], d3)
        for d2, d1 in itertools.product(range(2), repeat=2):
            landed[d1, d2, d3] = lax.ppermute(pieces[d1 * 2 + d2], AXES, route(d1, d2, d3))
    out = None
    for d3 in range(2):
        pieces = [landed[d1, d2, d3] for d1, d2 in itertools.product(range(2), repeat=2)]
        out = third_section(pieces, weights[2], d3, out)
    return out


def solution(mesh):
    fine = Mesh(mesh.devices.reshape((2,) * len(AXES)), AXES)
    split = P(None, AXES[:4], AXES[4:])
    return jax.shard_map(body, mesh=fine, in_specs=(split, P(), P()), out_specs=split, check_vma=False)
```
